32 devices in a mesh: ens: 2 (over y), space: 4 (over z), tm: 2 (over x), spin: 2 (over core).
Axes of the slice: x: 2, y: 2, z: 4, core: 2. Of those that a mesh axis runs over, the one named last changes fastest.
Arguments:
- eigvecs: bfloat16 [4, 2, 3, 8192, 128], P('tm', None, None, 'space'), may hold values from -6 to 6
- links: bfloat16 [4, 3, 2, 3, 3, 8192], P('tm', None, None, None, None, 'space'), may hold values from -2.5 to 2.5
- directions: int32 [4], P('spin'), may hold values from 0 to 3, each once
- pair_list: int32 [32, 2], P(('space', 'tm')), may hold values from 0 to 3
- pair_operators: int32 [32, 2], P(('space', 'tm')), may hold values from 0 to 3
- perambulators: bfloat16 [32, 16, 2, 128, 128], P(('space', 'tm'), 'spin'), may hold values from -0.5 to 0.5
Outputs:
- elementals: float32 [8, 4, 128, 2, 128], P(('ens', 'tm'), 'spin', 'space'), parts along dimension 0
- correlators: float32 [64, 2], P(('ens', 'space', 'tm')), parts along dimension 0
The draws below stay inside these ranges and needn't reach their ends.
There are 2 independent parts, one for each index of `ens`. The reference program is written for one: setup_inputs(seed, part) draws one part's arguments, and reference() takes and returns one part's arrays. A program takes and returns all parts, laid end to end along the dimension named above; an argument that names none is the same for every part. Nothing has to cross between parts.
Inputs may be any that keep to these rules, and one draw needn't show every extreme that they name: `directions`: each code once; 0, 1, 2 name a covariant derivative along the first, second and third spatial direction, 3 the eigenvectors with one unit of momentum along the third.
All inputs are finite; a program needn't handle non-finite values.
Results may differ from the reference program's by a relative error of at most 0.0071.
Values may be sent and summed in bfloat16 or wider, within the bound.
A program may use at most 128 MiB of HBM per device.

```python
import math
from functools import partial
import jax
import jax.numpy as jnp
from jax import lax

NEV = 128
SPIN_PAIRS = 16
NOPS = 4
PX = 16
PY = 16
ZB = 8
NT = 4
NSITES = 8192
NP = 32
N_SPACE = 4


def touch_ends(entries, stream_key, low, top_value):
    longest = entries.shape.index(max(entries.shape))
    spots = []
    for shift in (0, 1):
        where = [jax.random.randint(jax.random.fold_in(stream_key, axis), (), 0, length) for axis, length in enumerate(entries.shape)]
        where[longest] = (where[longest] + shift) % entries.shape[longest]
        spots.append(tuple(where))
    return entries.at[spots[0]].set(low).at[spots[1]].set(top_value)


def level_of(stream_key, shape, shards, smallest, top_value):
    def one(dim, blocks):
        draws = jax.random.uniform(jax.random.fold_in(jax.random.fold_in(stream_key, 6), dim), (blocks,), jnp.float32, smallest / len(shards), top_value / len(shards))
        return jnp.repeat(jnp.exp(draws), shape[dim] // blocks).reshape((-1,) + (1,) * (len(shape) - dim - 1))

    level = one(*shards[0])
    for cut in shards[1:]:
        level = level * one(*cut)
    return level


def centred(key, extent, width, reach, shards=(), held_as=jnp.bfloat16):
    loudness = level_of(key, extent, shards, -0.22, 0.18) if shards else 1.0
    entries = jax.random.normal(key, extent, jnp.float32) * width * loudness
    return jnp.minimum(jnp.maximum(entries, -reach), reach).astype(held_as)


def setup_inputs(seed: int = 0, part: int = 0) -> dict:
    seeds = jax.random.split(jax.random.key(seed), 7)
    return {
        "eigvecs": centred(seeds[0], (NT, 2, 3, NSITES, NEV), 1.0, 6.0, ((0, 2), (3, 4))),
        "links": centred(seeds[1], (NT, 3, 2, 3, 3, NSITES), 0.4, 2.5, ((0, 2), (5, 4))),
        "directions": jax.random.permutation(seeds[2], NOPS).astype(jnp.int32),
        "pair_list": touch_ends(jax.random.randint(seeds[3], (NP, 2), 0, NT), jax.random.fold_in(seeds[3], 1), 0, NT - 1).astype(jnp.int32),
        "pair_operators": touch_ends(jax.random.randint(seeds[4], (NP, 2), 0, NOPS), jax.random.fold_in(seeds[4], 1), 0, NOPS - 1).astype(jnp.int32),
        "perambulators": centred(seeds[5], (NP, SPIN_PAIRS, 2, NEV, NEV), NEV ** -0.5, 0.5, ((0, 8), (1, 2))),
    }


def apply_links(link_field, vectors):
    for b in range(3):
        link_real = link_field[0, :, b][..., None]
        link_imag = link_field[1, :, b][..., None]
        term_real = link_real * vectors[0, b] - link_imag * vectors[1, b]
        term_imag = link_real * vectors[1, b] + link_imag * vectors[0, b]
        if b == 0:
            total_real, total_imag = (term_real, term_imag)
        else:
            total_real, total_imag = (total_real + term_real, total_imag + term_imag)
    return jnp.stack([total_real, total_imag])

def apply_adjoint(link_field, vectors):
    for b in range(3):
        link_real = link_field[0, b][..., None]
        link_imag = link_field[1, b][..., None]
        term_real = link_real * vectors[0, b] + link_imag * vectors[1, b]
        term_imag = link_real * vectors[1, b] - link_imag * vectors[0, b]
        if b == 0:
            total_real, total_imag = (term_real, term_imag)
        else:
            total_real, total_imag = (total_real + term_real, total_imag + term_imag)
    return jnp.stack([total_real, total_imag])

def phase_field(vectors, z_coord, z_total):
    angles = 2.0 * math.pi / z_total * z_coord
    cosine_part = jnp.cos(angles)[:, None, None, None]
    sine_part = jnp.sin(angles)[:, None, None, None]
    return jnp.stack([cosine_part * vectors[0] + sine_part * vectors[1], cosine_part * vectors[1] - sine_part * vectors[0]])

def covariant(direction, vectors, link_field):
    roll_axis = 4 - direction
    links_along = link_field[direction]
    forward = apply_links(links_along, jnp.roll(vectors, -1, roll_axis))
    backward = jnp.roll(apply_adjoint(links_along, vectors), 1, roll_axis)
    return 0.5 * (forward - backward)

def gram_block(vectors_half, displaced, scaling):
    columns = vectors_half.shape[-1]
    left_side = vectors_half.reshape(-1, columns)
    displaced_half = displaced.astype(jnp.bfloat16)
    field_real = displaced_half[0].reshape(-1, columns)
    field_imag = displaced_half[1].reshape(-1, columns)
    right_side = jnp.concatenate([jnp.concatenate([field_real, field_imag], 0), jnp.concatenate([field_imag, -field_real], 0)], 1)
    product = lax.dot_general(left_side, right_side, (((0,), (0,)), ((), ())), preferred_element_type=jnp.float32)
    return (product * scaling).reshape(columns, 2, columns)

def contract_pair(source, sink_matrix, blocks, pair_signs):
    columns = source.shape[-1]
    sink_block = jnp.concatenate([jnp.concatenate([sink_matrix[:, 0], -sink_matrix[:, 1]], 1), jnp.concatenate([sink_matrix[:, 1], sink_matrix[:, 0]], 1)], 0)
    source_block = jnp.concatenate([jnp.concatenate([source[:, 0], source[:, 1]], 1), jnp.concatenate([-source[:, 1], source[:, 0]], 1)], 0)
    source_block = source_block.reshape(2, columns, 2 * columns)
    stacked = blocks.reshape(blocks.shape[0], 2 * columns, columns)
    halfway = jnp.einsum('mk,qkn->qmn', sink_block.astype(jnp.float32), stacked.astype(jnp.float32)).astype(jnp.bfloat16)
    second = jnp.einsum('qcmk,ckn->qmn', halfway.reshape(-1, 2, columns, columns).astype(jnp.float32), source_block.astype(jnp.float32))
    tau_real = blocks[:, 0].astype(jnp.float32)
    tau_imag = blocks[:, 1].astype(jnp.float32)
    out_real = second[:, :, :columns]
    out_imag = second[:, :, columns:]
    trace_real = lax.optimization_barrier(jnp.sum(out_real * tau_real + out_imag * tau_imag, axis=(1, 2)))
    trace_imag = lax.optimization_barrier(jnp.sum(out_imag * tau_real - out_real * tau_imag, axis=(1, 2)))
    return jnp.stack([jnp.sum(pair_signs * trace_real), jnp.sum(pair_signs * trace_imag)]) / (4.0 * columns)

def reference(eigvecs, links, directions, pair_list, pair_operators, perambulators):
    z_total = ZB * N_SPACE
    scaling = 1.0 / math.sqrt(6.0 * PX * PY * z_total)
    z_coord = jnp.arange(z_total).astype(jnp.float32)
    branches = [partial(covariant, 0), partial(covariant, 1), partial(covariant, 2), lambda vectors, link_field: phase_field(vectors, z_coord, z_total)]

    def per_slice(inputs):
        vectors_half, link_half = inputs
        vectors = vectors_half.astype(jnp.float32).reshape(2, 3, z_total, PY, PX, NEV)
        link_field = link_half.astype(jnp.float32).reshape(3, 2, 3, 3, z_total, PY, PX)
        blocks = []
        for op_slot in range(NOPS):
            displaced = lax.switch(directions[op_slot], branches, vectors, link_field)
            blocks.append(gram_block(vectors_half, displaced, scaling))
        return jnp.stack(blocks)
    elementals = lax.map(per_slice, (eigvecs, links))
    halves = elementals.astype(jnp.bfloat16)
    spin_signs = jnp.where(jnp.arange(4) < 2, 1.0, -1.0).astype(jnp.float32)
    pair_signs = (spin_signs[:, None] * spin_signs[None, :]).reshape(SPIN_PAIRS)

    def per_pair(inputs):
        time_pair, operator_pair, blocks = inputs
        source = halves[time_pair[0], operator_pair[0]]
        sink_matrix = halves[time_pair[1], operator_pair[1]]
        return contract_pair(source, sink_matrix, blocks, pair_signs)
    correlators = lax.map(per_pair, (pair_list, pair_operators, perambulators))
    return (elementals, correlators)
```

```python
import functools
import math

import jax
import jax.numpy as jnp
from jax import lax
from jax.experimental import pallas as pl
from jax.experimental.pallas import tpu as pltpu
from jax.sharding import PartitionSpec as P

PX = 16
PY = 16
PLANE = PX * PY
BF = jnp.bfloat16
F32 = jnp.float32


def neighbour_mask(group, shift_x):
    row = lax.broadcasted_iota(jnp.int32, (group, group), 0)
    col = lax.broadcasted_iota(jnp.int32, (group, group), 1)
    if shift_x:
        col = (col // PX) * PX + lax.rem(col + 1, PX)
    return jnp.where(row == col, 1.0, 0.0).astype(BF)


def carried(links_ref, lead, offset, group, mask, real, imag):
    columns = real[0].shape[-1]
    rows = []
    for b in range(3):
        parts = []
        for part in range(2):
            for a in range(3):
                row = links_ref[lead + (part, a, pl.ds(b, 1), pl.ds(offset, group))]
                parts.append(jnp.broadcast_to(row, (group, group)) * mask)
        rows.append(jnp.concatenate(parts, axis=1))
    matrix = jnp.concatenate(rows, axis=0)
    weights = jnp.concatenate(
        [jnp.concatenate([real[a], -imag[a]], axis=1) for a in range(3)]
        + [jnp.concatenate([imag[a], real[a]], axis=1) for a in range(3)],
        axis=0,
    )
    return jnp.dot(matrix, weights, preferred_element_type=F32).astype(BF)


def gram(left, right):
    return lax.dot_general(left, right, (((0,), (0,)), ((), ())), preferred_element_type=F32)


def antihermitian(product, columns, scaling):
    real = product[:columns, :columns] - product[columns:, columns:]
    imag = product[:columns, columns:] + product[columns:, :columns]
    return jnp.concatenate(
        [(0.5 * scaling) * (real - real.T), (0.5 * scaling) * (imag + imag.T)], axis=1
    )


def ones_where(condition):
    return jnp.where(condition, 1.0, 0.0).astype(BF)


def spread(row, mask):
    return jnp.broadcast_to(row, mask.shape) * mask


def stencil(forward, backward, mask_up, mask_down):
    def block(part, a, b):
        up = forward[part * 9 + a * 3 + b : part * 9 + a * 3 + b + 1]
        down = backward[part * 9 + b * 3 + a : part * 9 + b * 3 + a + 1]
        ahead = spread(up, mask_up) if mask_up is not None else None
        behind = spread(down if part else -down, mask_down) if mask_down is not None else None
        if ahead is None:
            return behind
        return ahead if behind is None else ahead + behind

    return jnp.concatenate(
        [
            jnp.concatenate([block(part, a, b) for part in range(2) for b in range(3)], axis=1)
            for a in range(3)
        ],
        axis=0,
    )


def local_kernel(
    plane_count, columns, scaling, dirs, phases, v_ref, links_ref, out_ref, flipped, moved
):
    code = dirs[pl.program_id(1)]
    group = PLANE // 2
    groups = plane_count * 2
    sites = plane_count * PLANE
    strip = group // plane_count

    @pl.when(pl.program_id(1) == 0)
    def _():
        def step(n, carry):
            start = pl.multiple_of(n * group, group)
            for part in range(2):
                for a in range(3):
                    flipped[
                        pl.ds(part * columns, columns),
                        pl.ds(pl.multiple_of(a * sites + start, group), group),
                    ] = v_ref[0, part, a, pl.ds(start, group), :].T
            return carry

        lax.fori_loop(0, groups, step, 0)

    def weights(rows):
        real = [rows(0, a) for a in range(3)]
        imag = [rows(1, a) for a in range(3)]
        return jnp.concatenate(
            [jnp.concatenate([real[a], imag[a]], axis=1) for a in range(3)]
            + [jnp.concatenate([-imag[a], real[a]], axis=1) for a in range(3)],
            axis=0,
        )

    row = lax.broadcasted_iota(jnp.int32, (group, group), 0)
    col = lax.broadcasted_iota(jnp.int32, (group, group), 1)

    def natural(start):
        return lambda part, a: v_ref[0, part, a, pl.ds(start, group), :]

    def keep(start, value):
        value = value.astype(BF)
        for a in range(3):
            moved[a, pl.ds(start, group), :] = value[a * group : (a + 1) * group]

    @pl.when(code == 0)
    def _():
        base = (col // PX) * PX
        within = col - base
        mask_up = ones_where(row == base + lax.rem(within + PX - 1, PX))
        mask_down = ones_where(row == base + lax.rem(within + 1, PX))
        lane = lax.broadcasted_iota(jnp.int32, (18, group), 1)

        def step(n, carry):
            start = pl.multiple_of(n * group, group)
            field = links_ref[0, 0, :, pl.ds(start, group)]
            ahead = jnp.where(
                lax.rem(lane, PX) == 0,
                pltpu.roll(field, group - PX + 1, 1),
                pltpu.roll(field, 1, 1),
            )
            matrix = stencil(ahead.astype(BF), field.astype(BF), mask_up, mask_down)
            keep(start, jnp.dot(matrix, weights(natural(start)), preferred_element_type=F32))
            return carry

        lax.fori_loop(0, groups, step, 0)

    @pl.when(code == 1)
    def _():
        mask_up = ones_where(row == col - PX)
        mask_down = ones_where(row == col + PX)
        edge_row = lax.broadcasted_iota(jnp.int32, (PX, group), 0)
        edge_col = lax.broadcasted_iota(jnp.int32, (PX, group), 1)
        edge_up = ones_where(edge_row == edge_col)
        edge_down = ones_where(edge_row == edge_col - (group - PX))

        def step(plane, carry):
            base = pl.multiple_of(plane * PLANE, PLANE)
            starts = [pl.multiple_of(base + half * group, group) for half in range(2)]
            fields = [links_ref[0, 0, :, pl.ds(start, group)] for start in starts]
            turned = [pltpu.roll(field, PX, 1).astype(BF) for field in fields]
            fields = [field.astype(BF) for field in fields]
            loaded = [weights(natural(start)) for start in starts]
            for half in range(2):
                far = 1 - half
                matrix = stencil(turned[half], fields[half], mask_up, mask_down)
                edge = jnp.concatenate(
                    [
                        stencil(turned[half], fields[far], None, edge_down),
                        stencil(turned[half], fields[far], edge_up, None),
                    ],
                    axis=0,
                )
                value = jnp.dot(matrix, loaded[half], preferred_element_type=F32)
                rim = jnp.dot(edge, loaded[far], preferred_element_type=F32)
                pieces = []
                for a in range(3):
                    low, high = a * group, (a + 1) * group
                    pieces += [
                        value[low : low + PX] + rim[a * PX : (a + 1) * PX],
                        value[low + PX : high - PX],
                        value[high - PX : high] + rim[(3 + a) * PX : (4 + a) * PX],
                    ]
                keep(starts[half], jnp.concatenate(pieces, axis=0))
            return carry

        lax.fori_loop(0, plane_count, step, 0)

    @pl.when(code == 2)
    def _():
        mask_up = ones_where(row == col - strip)
        mask_down = ones_where(row == col + strip)

        def step(n, carry):
            start = pl.multiple_of(n * group, group)
            field = links_ref[0, 0, :, pl.ds(start, group)]
            ahead = pltpu.roll(field, strip, 1)
            matrix = stencil(ahead.astype(BF), field.astype(BF), mask_up, mask_down)
            places = [
                pl.multiple_of(z * PLANE + n * strip, strip) for z in range(plane_count)
            ]
            loaded = weights(
                lambda part, a: jnp.concatenate(
                    [v_ref[0, part, a, pl.ds(place, strip), :] for place in places], axis=0
                )
            )
            value = jnp.dot(matrix, loaded, preferred_element_type=F32).astype(BF)
            for a in range(3):
                for z, place in enumerate(places):
                    low = a * group + z * strip
                    moved[a, pl.ds(place, strip), :] = value[low : low + strip]
            return carry

        lax.fori_loop(0, groups, step, 0)

    @pl.when(code == 3)
    def _():
        def step(plane, carry):
            base = pl.multiple_of(plane * PLANE, PLANE)
            cosine, sine = phases[0, plane], phases[1, plane]
            for a in range(3):
                real = v_ref[0, 0, a, pl.ds(base, PLANE), :].astype(F32)
                imag = v_ref[0, 1, a, pl.ds(base, PLANE), :].astype(F32)
                moved[a, pl.ds(base, PLANE), :] = jnp.concatenate(
                    [cosine * real + sine * imag, cosine * imag - sine * real], axis=1
                ).astype(BF)
            return carry

        lax.fori_loop(0, plane_count, step, 0)

    product = jnp.zeros((2 * columns, 2 * columns), F32)
    for a in range(3):
        product += jnp.dot(
            flipped[:, a * sites : (a + 1) * sites], moved[a], preferred_element_type=F32
        )
    scale = jnp.where(code == 3, scaling, 0.5 * scaling)
    out_ref[0, 0] = scale * jnp.concatenate(
        [
            product[:columns, :columns] + product[columns:, columns:],
            product[:columns, columns:] - product[columns:, :columns],
        ],
        axis=1,
    )


def boundary_kernel(columns, scaling, dirs, v_ref, links_ref, above_ref, part_ref, out_ref):
    op_slots = part_ref.shape[1]
    group = PLANE // 2
    for slot in range(op_slots):
        @pl.when(dirs[slot] != 2)
        def _(slot=slot):
            out_ref[0, slot] = part_ref[0, slot].astype(out_ref.dtype)

        @pl.when(dirs[slot] == 2)
        def _(slot=slot):
            mask = neighbour_mask(group, False)
            total = jnp.zeros((2 * columns, 2 * columns), F32)
            for half in range(2):
                own = [
                    [v_ref[0, p, a, pl.ds(half * group, group), :] for a in range(3)]
                    for p in range(2)
                ]
                moved = carried(links_ref, (0, 0), half * group, group, mask, *own)
                other = jnp.concatenate(
                    [
                        jnp.concatenate(
                            [
                                above_ref[0, p, a, pl.ds(half * group, group), :]
                                for p in range(2)
                            ],
                            axis=1,
                        )
                        for a in range(3)
                    ],
                    axis=0,
                )
                total += gram(moved, other)
            out_ref[0, slot] = (
                part_ref[0, slot] + antihermitian(total, columns, scaling)
            ).astype(out_ref.dtype)


def contract_kernel(columns, quarter, positions, signs, source_ref, sink_ref, tau_ref, out_ref):
    def whole(ref):
        value = ref[...].astype(F32)
        return value.reshape(columns, 2 * columns).astype(BF)

    source, sink = whole(source_ref), whole(sink_ref)
    count = tau_ref.shape[1]
    sr, si = sink[:, :columns], sink[:, columns:]
    sink_block = jnp.concatenate(
        [jnp.concatenate([sr, -si], axis=1), jnp.concatenate([si, sr], axis=1)], axis=0
    )
    rr, ri = source[:, :columns], source[:, columns:]
    source_block = jnp.concatenate(
        [jnp.concatenate([rr, ri], axis=1), jnp.concatenate([-ri, rr], axis=1)], axis=0
    )
    total_real = jnp.zeros((8, columns), F32)
    total_imag = jnp.zeros((8, columns), F32)
    for first in range(0, count, 2):
        some = range(first, min(first + 2, count))
        stacked = jnp.concatenate(
            [
                jnp.concatenate([tau_ref[0, q, 0], tau_ref[0, q, 1]], axis=0)
                for q in some
            ],
            axis=1,
        )
        halfway = jnp.dot(sink_block, stacked, preferred_element_type=F32).astype(BF)
        lines = jnp.concatenate(
            [
                jnp.concatenate(
                    [
                        halfway[:columns, n * columns : (n + 1) * columns],
                        halfway[columns:, n * columns : (n + 1) * columns],
                    ],
                    axis=1,
                )
                for n in range(len(some))
            ],
            axis=0,
        )
        second = jnp.dot(lines, source_block, preferred_element_type=F32)
        for n, q in enumerate(some):
            out_real = second[n * columns : (n + 1) * columns, :columns]
            out_imag = second[n * columns : (n + 1) * columns, columns:]
            tau_real = tau_ref[0, q, 0].astype(F32)
            tau_imag = tau_ref[0, q, 1].astype(F32)
            real = out_real * tau_real + out_imag * tau_imag
            imag = out_imag * tau_real - out_real * tau_imag
            total_real += signs[q] * jnp.sum(real.reshape(-1, 8, columns), axis=0)
            total_imag += signs[q] * jnp.sum(imag.reshape(-1, 8, columns), axis=0)
    out_ref[0, 0] = total_real
    out_ref[0, 1] = total_imag


def shift_over(array, axis, by):
    count = lax.axis_size(axis)
    return lax.ppermute(array, axis, [(i, (i + by) % count) for i in range(count)])


def halo(eigvecs):
    plane = eigvecs[:, :, :, :PLANE]
    if lax.axis_size("spin") != 2:
        return shift_over(plane, "space", -1)
    core = lax.axis_index("spin")
    mine = lax.dynamic_slice_in_dim(plane, core, 1, 1)
    mine = shift_over(mine, "space", -1)
    theirs = shift_over(mine, "spin", 1)
    return jnp.concatenate(
        [jnp.where(core == 0, mine, theirs), jnp.where(core == 0, theirs, mine)], axis=1
    )


def shards(eigvecs, links, directions, pair_list, pair_operators, perambulators):
    slices, _, _, local_sites, columns = eigvecs.shape
    plane_count = local_sites // PLANE
    layers = lax.axis_size("space")
    tm_size = lax.axis_size("tm")
    spin_size = lax.axis_size("spin")
    z_total = plane_count * layers
    scaling = 1.0 / math.sqrt(6.0 * PLANE * z_total)
    op_slots = directions.shape[0]
    z_coord = (lax.axis_index("space") * plane_count + jnp.arange(plane_count)).astype(F32)
    angles = 2.0 * math.pi / z_total * z_coord
    phases = jnp.stack([jnp.cos(angles), jnp.sin(angles)])
    above = halo(eigvecs)

    flat = links.astype(F32).reshape(slices, 3, 18, local_sites)
    strips = flat[:, 2].reshape(slices, 18, plane_count, -1, PLANE // 2 // plane_count)
    strips = jnp.swapaxes(strips, 2, 3).reshape(slices, 1, 18, local_sites)
    flat = jnp.concatenate([flat[:, :2], strips], axis=1)

    partial = pl.pallas_call(
        functools.partial(local_kernel, plane_count, columns, scaling),
        out_shape=jax.ShapeDtypeStruct((slices, op_slots, columns, 2 * columns), F32),
        grid_spec=pltpu.PrefetchScalarGridSpec(
            num_scalar_prefetch=2,
            grid=(slices, op_slots),
            in_specs=[
                pl.BlockSpec((1, 2, 3, local_sites, columns), lambda t, o, d, f: (t, 0, 0, 0, 0)),
                pl.BlockSpec(
                    (1, 1, 18, local_sites),
                    lambda t, o, d, f: (t, jnp.minimum(d[o], 2), 0, 0),
                ),
            ],
            out_specs=pl.BlockSpec((1, 1, columns, 2 * columns), lambda t, o, d, f: (t, o, 0, 0)),
            scratch_shapes=[
                pltpu.VMEM((2 * columns, 3 * local_sites), BF),
                pltpu.VMEM((3, local_sites, 2 * columns), BF),
            ],
        ),
        compiler_params=pltpu.CompilerParams(vmem_limit_bytes=48 << 20),
        cost_estimate=pl.CostEstimate(
            flops=13_000_000_000, bytes_accessed=eigvecs.size * 2, transcendentals=0
        ),
        name="local_gram",
    )(directions, phases, eigvecs, flat)

    last = plane_count - 1
    summed = pl.pallas_call(
        functools.partial(boundary_kernel, columns, scaling),
        out_shape=jax.ShapeDtypeStruct(partial.shape, F32),
        grid_spec=pltpu.PrefetchScalarGridSpec(
            num_scalar_prefetch=1,
            grid=(slices,),
            in_specs=[
                pl.BlockSpec((1, 2, 3, PLANE, columns), lambda t, d: (t, 0, 0, last, 0)),
                pl.BlockSpec((1, 1, 2, 3, 3, PLANE), lambda t, d: (t, 2, 0, 0, 0, last)),
                pl.BlockSpec((1, 2, 3, PLANE, columns), lambda t, d: (t, 0, 0, 0, 0)),
                pl.BlockSpec((1, op_slots, columns, 2 * columns), lambda t, d: (t, 0, 0, 0)),
            ],
            out_specs=pl.BlockSpec((1, op_slots, columns, 2 * columns), lambda t, d: (t, 0, 0, 0)),
        ),
        name="boundary",
    )(directions, eigvecs, links, above, partial)

    rows = columns // layers
    owned = lax.psum_scatter(summed, "space", scatter_dimension=2, tiled=True)
    elementals = owned.reshape(slices, op_slots, rows, 2, columns)
    table = lax.all_gather(owned.astype(BF), ("space", "tm", "spin"), axis=0)
    table = table.reshape(layers, tm_size * spin_size * slices * op_slots, rows, 2 * columns)

    position = (
        (pair_list // slices * spin_size + pair_operators // op_slots) * slices + pair_list % slices
    ) * op_slots + pair_operators % op_slots
    pair_count, count = perambulators.shape[0], perambulators.shape[1]
    spin_pair = lax.axis_index("spin") * count + jnp.arange(count)
    signs = jnp.where((spin_pair // 4 < 2) == (spin_pair % 4 < 2), 1.0, -1.0).astype(F32)
    block = (layers, 1, rows, 2 * columns)
    traces = pl.pallas_call(
        functools.partial(contract_kernel, columns, 4),
        out_shape=jax.ShapeDtypeStruct((pair_count, 2, 8, columns), F32),
        grid_spec=pltpu.PrefetchScalarGridSpec(
            num_scalar_prefetch=2,
            grid=(pair_count,),
            in_specs=[
                pl.BlockSpec(block, lambda p, pos, s: (0, pos[p, 0], 0, 0)),
                pl.BlockSpec(block, lambda p, pos, s: (0, pos[p, 1], 0, 0)),
                pl.BlockSpec((1, count, 2, columns, columns), lambda p, pos, s: (p, 0, 0, 0, 0)),
            ],
            out_specs=pl.BlockSpec((1, 2, 8, columns), lambda p, pos, s: (p, 0, 0, 0)),
        ),
        name="contract",
    )(position, signs, table, table, perambulators)
    part = jnp.sum(traces, axis=(2, 3)) / (4.0 * columns)
    if spin_size == 2:
        correlators = part + shift_over(part, "spin", 1)
    else:
        correlators = lax.psum(part, "spin")
    return (elementals, correlators)


def solution(mesh):
    return jax.shard_map(
        shards,
        mesh=mesh,
        in_specs=(
            P("tm", None, None, "space", None),
            P("tm", None, None, None, None, "space"),
            P("spin"),
            P(("space", "tm"), None),
            P(("space", "tm"), None),
            P(("space", "tm"), "spin", None, None, None),
        ),
        out_specs=(P(("ens", "tm"), "spin", "space", None, None), P(("ens", "space", "tm"), None)),
        check_vma=False,
    )
```

```python
import functools
import math

import jax
import jax.numpy as jnp
from jax import lax
from jax.experimental import pallas as pl
from jax.experimental.pallas import tpu as pltpu
from jax.sharding import PartitionSpec as P

PX = 16
PY = 16
PLANE = PX * PY
BF = jnp.bfloat16
F32 = jnp.float32
MESH = pl.DeviceIdType.MESH


def neighbour_mask(group, shift_x):
    row = lax.broadcasted_iota(jnp.int32, (group, group), 0)
    col = lax.broadcasted_iota(jnp.int32, (group, group), 1)
    if shift_x:
        col = (col // PX) * PX + lax.rem(col + 1, PX)
    return jnp.where(row == col, 1.0, 0.0).astype(BF)


def carried(links_ref, lead, offset, group, mask, real, imag):
    columns = real[0].shape[-1]
    rows = []
    for b in range(3):
        parts = []
        for part in range(2):
            for a in range(3):
                row = links_ref[lead + (part, a, pl.ds(b, 1), pl.ds(offset, group))]
                parts.append(jnp.broadcast_to(row, (group, group)) * mask)
        rows.append(jnp.concatenate(parts, axis=1))
    matrix = jnp.concatenate(rows, axis=0)
    weights = jnp.concatenate(
        [jnp.concatenate([real[a], -imag[a]], axis=1) for a in range(3)]
        + [jnp.concatenate([imag[a], real[a]], axis=1) for a in range(3)],
        axis=0,
    )
    return jnp.dot(matrix, weights, preferred_element_type=F32).astype(BF)


def gram(left, right):
    return lax.dot_general(left, right, (((0,), (0,)), ((), ())), preferred_element_type=F32)


def antihermitian(product, columns, scaling):
    real = product[:columns, :columns] - product[columns:, columns:]
    imag = product[:columns, columns:] + product[columns:, :columns]
    return jnp.concatenate(
        [(0.5 * scaling) * (real - real.T), (0.5 * scaling) * (imag + imag.T)], axis=1
    )


def ones_where(condition):
    return jnp.where(condition, 1.0, 0.0).astype(BF)


def spread(row, mask):
    return jnp.broadcast_to(row, mask.shape) * mask


def stencil(forward, backward, mask_up, mask_down):
    def block(part, a, b):
        up = forward[part * 9 + a * 3 + b : part * 9 + a * 3 + b + 1]
        down = backward[part * 9 + b * 3 + a : part * 9 + b * 3 + a + 1]
        ahead = spread(up, mask_up) if mask_up is not None else None
        behind = spread(down if part else -down, mask_down) if mask_down is not None else None
        if ahead is None:
            return behind
        return ahead if behind is None else ahead + behind

    return jnp.concatenate(
        [
            jnp.concatenate([block(part, a, b) for part in range(2) for b in range(3)], axis=1)
            for a in range(3)
        ],
        axis=0,
    )


def local_kernel(
    plane_count, columns, scaling, dirs, phases, v_ref, links_ref, out_ref, flipped, moved
):
    code = dirs[pl.program_id(1)]
    group = PLANE // 2
    groups = plane_count * 2
    sites = plane_count * PLANE
    strip = group // plane_count

    @pl.when(pl.program_id(1) == 0)
    def _():
        def step(n, carry):
            start = pl.multiple_of(n * group, group)
            for part in range(2):
                for a in range(3):
                    flipped[
                        pl.ds(part * columns, columns),
                        pl.ds(pl.multiple_of(a * sites + start, group), group),
                    ] = v_ref[0, part, a, pl.ds(start, group), :].T
            return carry

        lax.fori_loop(0, groups, step, 0)

    def weights(rows):
        real = [rows(0, a) for a in range(3)]
        imag = [rows(1, a) for a in range(3)]
        return jnp.concatenate(
            [jnp.concatenate([real[a], imag[a]], axis=1) for a in range(3)]
            + [jnp.concatenate([-imag[a], real[a]], axis=1) for a in range(3)],
            axis=0,
        )

    row = lax.broadcasted_iota(jnp.int32, (group, group), 0)
    col = lax.broadcasted_iota(jnp.int32, (group, group), 1)

    def natural(start):
        return lambda part, a: v_ref[0, part, a, pl.ds(start, group), :]

    def keep(start, value):
        value = value.astype(BF)
        for a in range(3):
            moved[a, pl.ds(start, group), :] = value[a * group : (a + 1) * group]

    @pl.when(code == 0)
    def _():
        base = (col // PX) * PX
        within = col - base
        mask_up = ones_where(row == base + lax.rem(within + PX - 1, PX))
        mask_down = ones_where(row == base + lax.rem(within + 1, PX))
        lane = lax.broadcasted_iota(jnp.int32, (18, group), 1)

        def step(n, carry):
            start = pl.multiple_of(n * group, group)
            field = links_ref[0, 0, :, pl.ds(start, group)]
            ahead = jnp.where(
                lax.rem(lane, PX) == 0,
                pltpu.roll(field, group - PX + 1, 1),
                pltpu.roll(field, 1, 1),
            )
            matrix = stencil(ahead.astype(BF), field.astype(BF), mask_up, mask_down)
            keep(start, jnp.dot(matrix, weights(natural(start)), preferred_element_type=F32))
            return carry

        lax.fori_loop(0, groups, step, 0)

    @pl.when(code == 1)
    def _():
        mask_up = ones_where(row == col - PX)
        mask_down = ones_where(row == col + PX)
        edge_row = lax.broadcasted_iota(jnp.int32, (PX, group), 0)
        edge_col = lax.broadcasted_iota(jnp.int32, (PX, group), 1)
        edge_up = ones_where(edge_row == edge_col)
        edge_down = ones_where(edge_row == edge_col - (group - PX))

        def step(plane, carry):
            base = pl.multiple_of(plane * PLANE, PLANE)
            starts = [pl.multiple_of(base + half * group, group) for half in range(2)]
            fields = [links_ref[0, 0, :, pl.ds(start, group)] for start in starts]
            turned = [pltpu.roll(field, PX, 1).astype(BF) for field in fields]
            fields = [field.astype(BF) for field in fields]
            loaded = [weights(natural(start)) for start in starts]
            for half in range(2):
                far = 1 - half
                matrix = stencil(turned[half], fields[half], mask_up, mask_down)
                edge = jnp.concatenate(
                    [
                        stencil(turned[half], fields[far], None, edge_down),
                        stencil(turned[half], fields[far], edge_up, None),
                    ],
                    axis=0,
                )
                value = jnp.dot(matrix, loaded[half], preferred_element_type=F32)
                rim = jnp.dot(edge, loaded[far], preferred_element_type=F32)
                pieces = []
                for a in range(3):
                    low, high = a * group, (a + 1) * group
                    pieces += [
                        value[low : low + PX] + rim[a * PX : (a + 1) * PX],
                        value[low + PX : high - PX],
                        value[high - PX : high] + rim[(3 + a) * PX : (4 + a) * PX],
                    ]
                keep(starts[half], jnp.concatenate(pieces, axis=0))
            return carry

        lax.fori_loop(0, plane_count, step, 0)

    @pl.when(code == 2)
    def _():
        mask_up = ones_where(row == col - strip)
        mask_down = ones_where(row == col + strip)

        def step(n, carry):
            start = pl.multiple_of(n * group, group)
            field = links_ref[0, 0, :, pl.ds(start, group)]
            ahead = pltpu.roll(field, strip, 1)
            matrix = stencil(ahead.astype(BF), field.astype(BF), mask_up, mask_down)
            places = [
                pl.multiple_of(z * PLANE + n * strip, strip) for z in range(plane_count)
            ]
            loaded = weights(
                lambda part, a: jnp.concatenate(
                    [v_ref[0, part, a, pl.ds(place, strip), :] for place in places], axis=0
                )
            )
            value = jnp.dot(matrix, loaded, preferred_element_type=F32).astype(BF)
            for a in range(3):
                for z, place in enumerate(places):
                    low = a * group + z * strip
                    moved[a, pl.ds(place, strip), :] = value[low : low + strip]
            return carry

        lax.fori_loop(0, groups, step, 0)

    @pl.when(code == 3)
    def _():
        def step(plane, carry):
            base = pl.multiple_of(plane * PLANE, PLANE)
            cosine, sine = phases[0, plane], phases[1, plane]
            for a in range(3):
                real = v_ref[0, 0, a, pl.ds(base, PLANE), :].astype(F32)
                imag = v_ref[0, 1, a, pl.ds(base, PLANE), :].astype(F32)
                moved[a, pl.ds(base, PLANE), :] = jnp.concatenate(
                    [cosine * real + sine * imag, cosine * imag - sine * real], axis=1
                ).astype(BF)
            return carry

        lax.fori_loop(0, plane_count, step, 0)

    product = jnp.zeros((2 * columns, 2 * columns), F32)
    for a in range(3):
        product += jnp.dot(
            flipped[:, a * sites : (a + 1) * sites], moved[a], preferred_element_type=F32
        )
    scale = jnp.where(code == 3, scaling, 0.5 * scaling)
    out_ref[0, 0] = scale * jnp.concatenate(
        [
            product[:columns, :columns] + product[columns:, columns:],
            product[:columns, columns:] - product[columns:, :columns],
        ],
        axis=1,
    )


def boundary_kernel(columns, scaling, dirs, v_ref, links_ref, above_ref, part_ref, out_ref):
    op_slots = part_ref.shape[1]
    group = PLANE // 2
    split = (out_ref.shape[0],) + out_ref.shape[3:]
    for slot in range(op_slots):
        @pl.when(dirs[slot] != 2)
        def _(slot=slot):
            out_ref[:, 0, slot] = part_ref[0, slot].reshape(split).astype(out_ref.dtype)

        @pl.when(dirs[slot] == 2)
        def _(slot=slot):
            mask = neighbour_mask(group, False)
            total = jnp.zeros((2 * columns, 2 * columns), F32)
            for half in range(2):
                own = [
                    [v_ref[0, p, a, pl.ds(half * group, group), :] for a in range(3)]
                    for p in range(2)
                ]
                moved = carried(links_ref, (0, 0), half * group, group, mask, *own)
                other = jnp.concatenate(
                    [
                        jnp.concatenate(
                            [
                                above_ref[0, p, a, pl.ds(half * group, group), :]
                                for p in range(2)
                            ],
                            axis=1,
                        )
                        for a in range(3)
                    ],
                    axis=0,
                )
                total += gram(moved, other)
            whole = part_ref[0, slot] + antihermitian(total, columns, scaling)
            out_ref[:, 0, slot] = whole.reshape(split).astype(out_ref.dtype)


def contract_kernel(columns, quarter, positions, signs, source_ref, sink_ref, tau_ref, out_ref):
    def whole(ref):
        value = ref[...].astype(F32)
        return value.reshape(columns, 2 * columns).astype(BF)

    source, sink = whole(source_ref), whole(sink_ref)
    count = tau_ref.shape[1]
    sr, si = sink[:, :columns], sink[:, columns:]
    sink_block = jnp.concatenate(
        [jnp.concatenate([sr, -si], axis=1), jnp.concatenate([si, sr], axis=1)], axis=0
    )
    rr, ri = source[:, :columns], source[:, columns:]
    source_block = jnp.concatenate(
        [jnp.concatenate([rr, ri], axis=1), jnp.concatenate([-ri, rr], axis=1)], axis=0
    )
    total_real = jnp.zeros((8, columns), F32)
    total_imag = jnp.zeros((8, columns), F32)
    for first in range(0, count, 2):
        some = range(first, min(first + 2, count))
        stacked = jnp.concatenate(
            [
                jnp.concatenate([tau_ref[0, q, 0], tau_ref[0, q, 1]], axis=0)
                for q in some
            ],
            axis=1,
        )
        halfway = jnp.dot(sink_block, stacked, preferred_element_type=F32).astype(BF)
        lines = jnp.concatenate(
            [
                jnp.concatenate(
                    [
                        halfway[:columns, n * columns : (n + 1) * columns],
                        halfway[columns:, n * columns : (n + 1) * columns],
                    ],
                    axis=1,
                )
                for n in range(len(some))
            ],
            axis=0,
        )
        second = jnp.dot(lines, source_block, preferred_element_type=F32)
        for n, q in enumerate(some):
            out_real = second[n * columns : (n + 1) * columns, :columns]
            out_imag = second[n * columns : (n + 1) * columns, columns:]
            tau_real = tau_ref[0, q, 0].astype(F32)
            tau_imag = tau_ref[0, q, 1].astype(F32)
            real = out_real * tau_real + out_imag * tau_imag
            imag = out_imag * tau_real - out_real * tau_imag
            total_real += signs[q] * jnp.sum(real.reshape(-1, 8, columns), axis=0)
            total_imag += signs[q] * jnp.sum(imag.reshape(-1, 8, columns), axis=0)
    out_ref[0, 0] = total_real
    out_ref[0, 1] = total_imag


def reduce_kernel(layers, in_ref, sum_ref, half_ref, held, send_sem, recv_sem):
    me = lax.axis_index("space")
    barrier = pltpu.get_barrier_semaphore()
    for d in range(1, layers):
        pl.semaphore_signal(
            barrier, inc=1, device_id={"space": lax.rem(me + d, layers)}, device_id_type=MESH
        )
    pl.semaphore_wait(barrier, layers - 1)
    copies = []
    for d in range(1, layers):
        peer = lax.rem(me + d, layers)
        copy = pltpu.make_async_remote_copy(
            src_ref=in_ref.at[peer],
            dst_ref=held.at[d - 1],
            send_sem=send_sem.at[d - 1],
            recv_sem=recv_sem.at[d - 1],
            device_id={"space": peer},
            device_id_type=MESH,
        )
        copy.start()
        copies.append(copy)
    total = in_ref[me]
    for d in range(1, layers):
        copies[d - 1].wait_recv()
        total += held[d - 1]
    sum_ref[...] = total
    half_ref[...] = total.astype(BF)
    for copy in copies:
        copy.wait_send()


def reduce_rows(blocks, layers):
    shape = blocks.shape[1:]
    return pl.pallas_call(
        functools.partial(reduce_kernel, layers),
        out_shape=(jax.ShapeDtypeStruct(shape, F32), jax.ShapeDtypeStruct(shape, BF)),
        in_specs=[pl.BlockSpec(memory_space=pltpu.VMEM)],
        out_specs=(pl.BlockSpec(memory_space=pltpu.VMEM),) * 2,
        scratch_shapes=[
            pltpu.VMEM((layers - 1,) + shape, F32),
            pltpu.SemaphoreType.DMA((layers - 1,)),
            pltpu.SemaphoreType.DMA((layers - 1,)),
        ],
        compiler_params=pltpu.CompilerParams(collective_id=0, has_side_effects=True),
        name="reduce_rows",
    )(blocks)


def gather_kernel(
    layers, times, cores, in_ref, out_ref, z_send, z_recv, t_send, t_recv, c_send, c_recv
):
    sizes = {"space": layers, "tm": times, "spin": cores}
    here = {axis: lax.axis_index(axis) for axis in sizes}
    barrier = pltpu.get_barrier_semaphore()
    for axis, size in sizes.items():
        for d in range(1, size):
            pl.semaphore_signal(
                barrier,
                inc=1,
                device_id={axis: lax.rem(here[axis] + d, size)},
                device_id_type=MESH,
            )
    pl.semaphore_wait(barrier, layers + times + cores - 3)

    def slot(d, e):
        z = lax.rem(here["space"] + layers - d, layers)
        t = lax.rem(here["tm"] + times - e, times)
        return out_ref.at[z, t, here["spin"]]

    def send(axis, distance, d, e, send_sem, recv_sem):
        size = sizes[axis]
        copy = pltpu.make_async_remote_copy(
            src_ref=in_ref if d == 0 and e == 0 else slot(d, e),
            dst_ref=slot(d, e),
            send_sem=send_sem,
            recv_sem=recv_sem,
            device_id={axis: lax.rem(here[axis] + distance, size)},
            device_id_type=MESH,
        )
        copy.start()
        return copy

    z_copies = [
        send("space", d, 0, 0, z_send.at[d], z_recv.at[d]) for d in range(1, layers)
    ]
    t_copies, c_copies = {}, []

    def pass_cores(d, e):
        for f in range(1, cores):
            c_copies.append(send("spin", f, d, e, c_send.at[d, e, f], c_recv.at[d, e, f]))

    def pass_times(d):
        for e in range(1, times):
            t_copies[d, e] = send("tm", e, d, 0, t_send.at[d, e], t_recv.at[d, e])
        pass_cores(d, 0)

    pass_times(0)
    out_ref[here["space"], here["tm"], here["spin"]] = in_ref[...]
    for d in range(1, layers):
        z_copies[d - 1].wait_recv()
        pass_times(d)
    for (d, e), copy in t_copies.items():
        copy.wait_recv()
        pass_cores(d, e)
    for copy in c_copies:
        copy.wait()
    for copy in z_copies + list(t_copies.values()):
        copy.wait_send()


def gather_all(block, layers, times, cores):
    dma = pltpu.SemaphoreType.DMA
    return pl.pallas_call(
        functools.partial(gather_kernel, layers, times, cores),
        out_shape=jax.ShapeDtypeStruct((layers, times, cores) + block.shape, BF),
        in_specs=[pl.BlockSpec(memory_space=pltpu.VMEM)],
        out_specs=pl.BlockSpec(memory_space=pltpu.VMEM),
        scratch_shapes=[
            dma((layers,)),
            dma((layers,)),
            dma((layers, times)),
            dma((layers, times)),
            dma((layers, times, cores)),
            dma((layers, times, cores)),
        ],
        compiler_params=pltpu.CompilerParams(collective_id=1, has_side_effects=True),
        name="gather_all",
    )(block)


def shift_over(array, axis, by):
    count = lax.axis_size(axis)
    return lax.ppermute(array, axis, [(i, (i + by) % count) for i in range(count)])


def halo(eigvecs):
    plane = eigvecs[:, :, :, :PLANE]
    if lax.axis_size("spin") != 2:
        return shift_over(plane, "space", -1)
    core = lax.axis_index("spin")
    mine = lax.dynamic_slice_in_dim(plane, core, 1, 1)
    mine = shift_over(mine, "space", -1)
    theirs = shift_over(mine, "spin", 1)
    return jnp.concatenate(
        [jnp.where(core == 0, mine, theirs), jnp.where(core == 0, theirs, mine)], axis=1
    )


def shards(eigvecs, links, directions, pair_list, pair_operators, perambulators):
    slices, _, _, local_sites, columns = eigvecs.shape
    plane_count = local_sites // PLANE
    layers = lax.axis_size("space")
    tm_size = lax.axis_size("tm")
    spin_size = lax.axis_size("spin")
    z_total = plane_count * layers
    scaling = 1.0 / math.sqrt(6.0 * PLANE * z_total)
    op_slots = directions.shape[0]
    z_coord = (lax.axis_index("space") * plane_count + jnp.arange(plane_count)).astype(F32)
    angles = 2.0 * math.pi / z_total * z_coord
    phases = jnp.stack([jnp.cos(angles), jnp.sin(angles)])
    above = halo(eigvecs)

    flat = links.astype(F32).reshape(slices, 3, 18, local_sites)
    strips = flat[:, 2].reshape(slices, 18, plane_count, -1, PLANE // 2 // plane_count)
    strips = jnp.swapaxes(strips, 2, 3).reshape(slices, 1, 18, local_sites)
    flat = jnp.concatenate([flat[:, :2], strips], axis=1)

    partial = pl.pallas_call(
        functools.partial(local_kernel, plane_count, columns, scaling),
        out_shape=jax.ShapeDtypeStruct((slices, op_slots, columns, 2 * columns), F32),
        grid_spec=pltpu.PrefetchScalarGridSpec(
            num_scalar_prefetch=2,
            grid=(slices, op_slots),
            in_specs=[
                pl.BlockSpec((1, 2, 3, local_sites, columns), lambda t, o, d, f: (t, 0, 0, 0, 0)),
                pl.BlockSpec(
                    (1, 1, 18, local_sites),
                    lambda t, o, d, f: (t, jnp.minimum(d[o], 2), 0, 0),
                ),
            ],
            out_specs=pl.BlockSpec((1, 1, columns, 2 * columns), lambda t, o, d, f: (t, o, 0, 0)),
            scratch_shapes=[
                pltpu.VMEM((2 * columns, 3 * local_sites), BF),
                pltpu.VMEM((3, local_sites, 2 * columns), BF),
            ],
        ),
        compiler_params=pltpu.CompilerParams(vmem_limit_bytes=48 << 20),
        cost_estimate=pl.CostEstimate(
            flops=13_000_000_000, bytes_accessed=eigvecs.size * 2, transcendentals=0
        ),
        name="local_gram",
    )(directions, phases, eigvecs, flat)

    last = plane_count - 1
    rows = columns // layers
    summed = pl.pallas_call(
        functools.partial(boundary_kernel, columns, scaling),
        out_shape=jax.ShapeDtypeStruct((layers, slices, op_slots, rows, 2 * columns), F32),
        grid_spec=pltpu.PrefetchScalarGridSpec(
            num_scalar_prefetch=1,
            grid=(slices,),
            in_specs=[
                pl.BlockSpec((1, 2, 3, PLANE, columns), lambda t, d: (t, 0, 0, last, 0)),
                pl.BlockSpec((1, 1, 2, 3, 3, PLANE), lambda t, d: (t, 2, 0, 0, 0, last)),
                pl.BlockSpec((1, 2, 3, PLANE, columns), lambda t, d: (t, 0, 0, 0, 0)),
                pl.BlockSpec((1, op_slots, columns, 2 * columns), lambda t, d: (t, 0, 0, 0)),
            ],
            out_specs=pl.BlockSpec(
                (layers, 1, op_slots, rows, 2 * columns), lambda t, d: (0, t, 0, 0, 0)
            ),
        ),
        name="boundary",
    )(directions, eigvecs, links, above, partial)

    elementals, halves = reduce_rows(summed, layers)
    elementals = elementals.reshape(slices, op_slots, rows, 2, columns)
    table = gather_all(halves, layers, tm_size, spin_size)
    table = table.reshape(layers, tm_size * spin_size * slices * op_slots, rows, 2 * columns)

    position = (
        (pair_list // slices * spin_size + pair_operators // op_slots) * slices + pair_list % slices
    ) * op_slots + pair_operators % op_slots
    pair_count, count = perambulators.shape[0], perambulators.shape[1]
    spin_pair = lax.axis_index("spin") * count + jnp.arange(count)
    signs = jnp.where((spin_pair // 4 < 2) == (spin_pair % 4 < 2), 1.0, -1.0).astype(F32)
    block = (layers, 1, rows, 2 * columns)
    traces = pl.pallas_call(
        functools.partial(contract_kernel, columns, 4),
        out_shape=jax.ShapeDtypeStruct((pair_count, 2, 8, columns), F32),
        grid_spec=pltpu.PrefetchScalarGridSpec(
            num_scalar_prefetch=2,
            grid=(pair_count,),
            in_specs=[
                pl.BlockSpec(block, lambda p, pos, s: (0, pos[p, 0], 0, 0)),
                pl.BlockSpec(block, lambda p, pos, s: (0, pos[p, 1], 0, 0)),
                pl.BlockSpec((1, count, 2, columns, columns), lambda p, pos, s: (p, 0, 0, 0, 0)),
            ],
            out_specs=pl.BlockSpec((1, 2, 8, columns), lambda p, pos, s: (p, 0, 0, 0)),
        ),
        name="contract",
    )(position, signs, table, table, perambulators)
    part = jnp.sum(traces, axis=(2, 3)) / (4.0 * columns)
    if spin_size == 2:
        correlators = part + shift_over(part, "spin", 1)
    else:
        correlators = lax.psum(part, "spin")
    return (elementals, correlators)


def solution(mesh):
    return jax.shard_map(
        shards,
        mesh=mesh,
        in_specs=(
            P("tm", None, None, "space", None),
            P("tm", None, None, None, None, "space"),
            P("spin"),
            P(("space", "tm"), None),
            P(("space", "tm"), None),
            P(("space", "tm"), "spin", None, None, None),
        ),
        out_specs=(P(("ens", "tm"), "spin", "space", None, None), P(("ens", "space", "tm"), None)),
        check_vma=False,
    )
```

```python
import functools
import math

import jax
import jax.numpy as jnp
from jax import lax
from jax.experimental import pallas as pl
from jax.experimental.pallas import tpu as pltpu
from jax.sharding import PartitionSpec as P

PX = 16
PY = 16
PLANE = PX * PY
BF = jnp.bfloat16
F32 = jnp.float32
MESH = pl.DeviceIdType.MESH


def neighbour_mask(group, shift_x):
    row = lax.broadcasted_iota(jnp.int32, (group, group), 0)
    col = lax.broadcasted_iota(jnp.int32, (group, group), 1)
    if shift_x:
        col = (col // PX) * PX + lax.rem(col + 1, PX)
    return jnp.where(row == col, 1.0, 0.0).astype(BF)


def carried(links_ref, lead, offset, group, mask, real, imag):
    columns = real[0].shape[-1]
    rows = []
    for b in range(3):
        parts = []
        for part in range(2):
            for a in range(3):
                row = links_ref[lead + (part, a, pl.ds(b, 1), pl.ds(offset, group))]
                parts.append(jnp.broadcast_to(row, (group, group)) * mask)
        rows.append(jnp.concatenate(parts, axis=1))
    matrix = jnp.concatenate(rows, axis=0)
    weights = jnp.concatenate(
        [jnp.concatenate([real[a], -imag[a]], axis=1) for a in range(3)]
        + [jnp.concatenate([imag[a], real[a]], axis=1) for a in range(3)],
        axis=0,
    )
    return jnp.dot(matrix, weights, preferred_element_type=F32).astype(BF)


def gram(left, right):
    return lax.dot_general(left, right, (((0,), (0,)), ((), ())), preferred_element_type=F32)


def antihermitian(product, columns, scaling):
    real = product[:columns, :columns] - product[columns:, columns:]
    imag = product[:columns, columns:] + product[columns:, :columns]
    return jnp.concatenate(
        [(0.5 * scaling) * (real - real.T), (0.5 * scaling) * (imag + imag.T)], axis=1
    )


def ones_where(condition):
    return jnp.where(condition, 1.0, 0.0).astype(BF)


def spread(row, mask):
    return jnp.broadcast_to(row, mask.shape) * mask


def stencil(forward, backward, mask_up, mask_down):
    def block(part, a, b):
        up = forward[part * 9 + a * 3 + b : part * 9 + a * 3 + b + 1]
        down = backward[part * 9 + b * 3 + a : part * 9 + b * 3 + a + 1]
        ahead = spread(up, mask_up) if mask_up is not None else None
        behind = spread(down if part else -down, mask_down) if mask_down is not None else None
        if ahead is None:
            return behind
        return ahead if behind is None else ahead + behind

    return jnp.concatenate(
        [
            jnp.concatenate([block(part, a, b) for part in range(2) for b in range(3)], axis=1)
            for a in range(3)
        ],
        axis=0,
    )


def local_kernel(
    plane_count, columns, scaling, dirs, phases, v_ref, links_ref, out_ref, flipped, moved
):
    code = dirs[pl.program_id(1)]
    group = PLANE // 2
    groups = plane_count * 2
    sites = plane_count * PLANE
    strip = group // plane_count

    @pl.when(pl.program_id(1) == 0)
    def _():
        def step(n, carry):
            start = pl.multiple_of(n * group, group)
            for part in range(2):
                for a in range(3):
                    flipped[
                        pl.ds(part * columns, columns),
                        pl.ds(pl.multiple_of(a * sites + start, group), group),
                    ] = v_ref[0, part, a, pl.ds(start, group), :].T
            return carry

        lax.fori_loop(0, groups, step, 0)

    def weights(rows):
        real = [rows(0, a) for a in range(3)]
        imag = [rows(1, a) for a in range(3)]
        return jnp.concatenate(
            [jnp.concatenate([real[a], imag[a]], axis=1) for a in range(3)]
            + [jnp.concatenate([-imag[a], real[a]], axis=1) for a in range(3)],
            axis=0,
        )

    row = lax.broadcasted_iota(jnp.int32, (group, group), 0)
    col = lax.broadcasted_iota(jnp.int32, (group, group), 1)

    def natural(start):
        return lambda part, a: v_ref[0, part, a, pl.ds(start, group), :]

    def keep(start, value):
        value = value.astype(BF)
        for a in range(3):
            moved[a, pl.ds(start, group), :] = value[a * group : (a + 1) * group]

    @pl.when(code == 0)
    def _():
        base = (col // PX) * PX
        within = col - base
        mask_up = ones_where(row == base + lax.rem(within + PX - 1, PX))
        mask_down = ones_where(row == base + lax.rem(within + 1, PX))
        lane = lax.broadcasted_iota(jnp.int32, (18, group), 1)

        def step(n, carry):
            start = pl.multiple_of(n * group, group)
            field = links_ref[0, 0, :, pl.ds(start, group)]
            ahead = jnp.where(
                lax.rem(lane, PX) == 0,
                pltpu.roll(field, group - PX + 1, 1),
                pltpu.roll(field, 1, 1),
            )
            matrix = stencil(ahead.astype(BF), field.astype(BF), mask_up, mask_down)
            keep(start, jnp.dot(matrix, weights(natural(start)), preferred_element_type=F32))
            return carry

        lax.fori_loop(0, groups, step, 0)

    @pl.when(code == 1)
    def _():
        mask_up = ones_where(row == col - PX)
        mask_down = ones_where(row == col + PX)
        edge_row = lax.broadcasted_iota(jnp.int32, (PX, group), 0)
        edge_col = lax.broadcasted_iota(jnp.int32, (PX, group), 1)
        edge_up = ones_where(edge_row == edge_col)
        edge_down = ones_where(edge_row == edge_col - (group - PX))

        def step(plane, carry):
            base = pl.multiple_of(plane * PLANE, PLANE)
            starts = [pl.multiple_of(base + half * group, group) for half in range(2)]
            fields = [links_ref[0, 0, :, pl.ds(start, group)] for start in starts]
            turned = [pltpu.roll(field, PX, 1).astype(BF) for field in fields]
            fields = [field.astype(BF) for field in fields]
            loaded = [weights(natural(start)) for start in starts]
            for half in range(2):
                far = 1 - half
                matrix = stencil(turned[half], fields[half], mask_up, mask_down)
                edge = jnp.concatenate(
                    [
                        stencil(turned[half], fields[far], None, edge_down),
                        stencil(turned[half], fields[far], edge_up, None),
                    ],
                    axis=0,
                )
                value = jnp.dot(matrix, loaded[half], preferred_element_type=F32)
                rim = jnp.dot(edge, loaded[far], preferred_element_type=F32)
                pieces = []
                for a in range(3):
                    low, high = a * group, (a + 1) * group
                    pieces += [
                        value[low : low + PX] + rim[a * PX : (a + 1) * PX],
                        value[low + PX : high - PX],
                        value[high - PX : high] + rim[(3 + a) * PX : (4 + a) * PX],
                    ]
                keep(starts[half], jnp.concatenate(pieces, axis=0))
            return carry

        lax.fori_loop(0, plane_count, step, 0)

    @pl.when(code == 2)
    def _():
        lane = lax.broadcasted_iota(jnp.int32, (18, group), 1)
        mask_up = ones_where(row == col - strip)
        mask_down = ones_where(row == col + strip)

        def step(n, carry):
            per_chunk = group // strip
            chunk = pl.multiple_of((n // per_chunk) * group, group)
            turn = lax.rem(n, per_chunk)
            field = jnp.zeros((18, group), F32)
            for z in range(plane_count):
                line = links_ref[0, 0, :, pl.ds(z * PLANE + chunk, group)]
                shift = lax.rem(z + per_chunk - turn, per_chunk) * strip
                field = jnp.where(lane // strip == z, pltpu.roll(line, shift, 1), field)
            ahead = pltpu.roll(field, strip, 1)
            matrix = stencil(ahead.astype(BF), field.astype(BF), mask_up, mask_down)
            places = [
                pl.multiple_of(z * PLANE + n * strip, strip) for z in range(plane_count)
            ]
            loaded = weights(
                lambda part, a: jnp.concatenate(
                    [v_ref[0, part, a, pl.ds(place, strip), :] for place in places], axis=0
                )
            )
            value = jnp.dot(matrix, loaded, preferred_element_type=F32).astype(BF)
            for a in range(3):
                for z, place in enumerate(places):
                    low = a * group + z * strip
                    moved[a, pl.ds(place, strip), :] = value[low : low + strip]
            return carry

        lax.fori_loop(0, groups, step, 0)

    @pl.when(code == 3)
    def _():
        def step(plane, carry):
            base = pl.multiple_of(plane * PLANE, PLANE)
            cosine, sine = phases[0, plane], phases[1, plane]
            for a in range(3):
                real = v_ref[0, 0, a, pl.ds(base, PLANE), :].astype(F32)
                imag = v_ref[0, 1, a, pl.ds(base, PLANE), :].astype(F32)
                moved[a, pl.ds(base, PLANE), :] = jnp.concatenate(
                    [cosine * real + sine * imag, cosine * imag - sine * real], axis=1
                ).astype(BF)
            return carry

        lax.fori_loop(0, plane_count, step, 0)

    product = jnp.zeros((2 * columns, 2 * columns), F32)
    for a in range(3):
        product += jnp.dot(
            flipped[:, a * sites : (a + 1) * sites], moved[a], preferred_element_type=F32
        )
    scale = jnp.where(code == 3, scaling, 0.5 * scaling)
    out_ref[0, 0] = scale * jnp.concatenate(
        [
            product[:columns, :columns] + product[columns:, columns:],
            product[:columns, columns:] - product[columns:, :columns],
        ],
        axis=1,
    )


def boundary_kernel(columns, scaling, dirs, v_ref, links_ref, above_ref, part_ref, out_ref):
    op_slots = part_ref.shape[1]
    group = PLANE // 2
    split = (out_ref.shape[0],) + out_ref.shape[3:]
    for slot in range(op_slots):
        @pl.when(dirs[slot] != 2)
        def _(slot=slot):
            out_ref[:, 0, slot] = part_ref[0, slot].reshape(split).astype(out_ref.dtype)

        @pl.when(dirs[slot] == 2)
        def _(slot=slot):
            mask = neighbour_mask(group, False)
            total = jnp.zeros((2 * columns, 2 * columns), F32)
            for half in range(2):
                own = [
                    [v_ref[0, p, a, pl.ds(half * group, group), :] for a in range(3)]
                    for p in range(2)
                ]
                moved = carried(links_ref, (0, 0), half * group, group, mask, *own)
                other = jnp.concatenate(
                    [
                        jnp.concatenate(
                            [
                                above_ref[0, p, a, pl.ds(half * group, group), :]
                                for p in range(2)
                            ],
                            axis=1,
                        )
                        for a in range(3)
                    ],
                    axis=0,
                )
                total += gram(moved, other)
            whole = part_ref[0, slot] + antihermitian(total, columns, scaling)
            out_ref[:, 0, slot] = whole.reshape(split).astype(out_ref.dtype)


def contract_kernel(columns, quarter, positions, signs, source_ref, sink_ref, tau_ref, out_ref):
    def whole(ref):
        value = ref[...].astype(F32)
        return value.reshape(columns, 2 * columns).astype(BF)

    source, sink = whole(source_ref), whole(sink_ref)
    count = tau_ref.shape[1]
    sr, si = sink[:, :columns], sink[:, columns:]
    sink_block = jnp.concatenate(
        [jnp.concatenate([sr, -si], axis=1), jnp.concatenate([si, sr], axis=1)], axis=0
    )
    rr, ri = source[:, :columns], source[:, columns:]
    source_block = jnp.concatenate(
        [jnp.concatenate([rr, ri], axis=1), jnp.concatenate([-ri, rr], axis=1)], axis=0
    )
    total_real = jnp.zeros((8, columns), F32)
    total_imag = jnp.zeros((8, columns), F32)
    for first in range(0, count, 2):
        some = range(first, min(first + 2, count))
        stacked = jnp.concatenate(
            [
                jnp.concatenate([tau_ref[0, q, 0], tau_ref[0, q, 1]], axis=0)
                for q in some
            ],
            axis=1,
        )
        halfway = jnp.dot(sink_block, stacked, preferred_element_type=F32).astype(BF)
        lines = jnp.concatenate(
            [
                jnp.concatenate(
                    [
                        halfway[:columns, n * columns : (n + 1) * columns],
                        halfway[columns:, n * columns : (n + 1) * columns],
                    ],
                    axis=1,
                )
                for n in range(len(some))
            ],
            axis=0,
        )
        second = jnp.dot(lines, source_block, preferred_element_type=F32)
        for n, q in enumerate(some):
            out_real = second[n * columns : (n + 1) * columns, :columns]
            out_imag = second[n * columns : (n + 1) * columns, columns:]
            tau_real = tau_ref[0, q, 0].astype(F32)
            tau_imag = tau_ref[0, q, 1].astype(F32)
            real = out_real * tau_real + out_imag * tau_imag
            imag = out_imag * tau_real - out_real * tau_imag
            total_real += signs[q] * jnp.sum(real.reshape(-1, 8, columns), axis=0)
            total_imag += signs[q] * jnp.sum(imag.reshape(-1, 8, columns), axis=0)
    out_ref[0, 0] = total_real
    out_ref[0, 1] = total_imag


def reduce_kernel(layers, in_ref, sum_ref, half_ref, held, send_sem, recv_sem):
    me = lax.axis_index("space")
    barrier = pltpu.get_barrier_semaphore()
    for d in range(1, layers):
        pl.semaphore_signal(
            barrier, inc=1, device_id={"space": lax.rem(me + d, layers)}, device_id_type=MESH
        )
    pl.semaphore_wait(barrier, layers - 1)
    copies = []
    for d in range(1, layers):
        peer = lax.rem(me + d, layers)
        copy = pltpu.make_async_remote_copy(
            src_ref=in_ref.at[peer],
            dst_ref=held.at[d - 1],
            send_sem=send_sem.at[d - 1],
            recv_sem=recv_sem.at[d - 1],
            device_id={"space": peer},
            device_id_type=MESH,
        )
        copy.start()
        copies.append(copy)
    total = in_ref[me]
    for d in range(1, layers):
        copies[d - 1].wait_recv()
        total += held[d - 1]
    sum_ref[...] = total
    half_ref[...] = total.astype(BF)
    for copy in copies:
        copy.wait_send()


def reduce_rows(blocks, layers):
    shape = blocks.shape[1:]
    return pl.pallas_call(
        functools.partial(reduce_kernel, layers),
        out_shape=(jax.ShapeDtypeStruct(shape, F32), jax.ShapeDtypeStruct(shape, BF)),
        in_specs=[pl.BlockSpec(memory_space=pltpu.VMEM)],
        out_specs=(pl.BlockSpec(memory_space=pltpu.VMEM),) * 2,
        scratch_shapes=[
            pltpu.VMEM((layers - 1,) + shape, F32),
            pltpu.SemaphoreType.DMA((layers - 1,)),
            pltpu.SemaphoreType.DMA((layers - 1,)),
        ],
        compiler_params=pltpu.CompilerParams(collective_id=0, has_side_effects=True),
        name="reduce_rows",
    )(blocks)


def gather_kernel(
    layers, times, cores, in_ref, out_ref, z_send, z_recv, t_send, t_recv, c_send, c_recv
):
    sizes = {"space": layers, "tm": times, "spin": cores}
    here = {axis: lax.axis_index(axis) for axis in sizes}
    barrier = pltpu.get_barrier_semaphore()
    for axis, size in sizes.items():
        for d in range(1, size):
            pl.semaphore_signal(
                barrier,
                inc=1,
                device_id={axis: lax.rem(here[axis] + d, size)},
                device_id_type=MESH,
            )
    pl.semaphore_wait(barrier, layers + times + cores - 3)

    def slot(d, e):
        z = lax.rem(here["space"] + layers - d, layers)
        t = lax.rem(here["tm"] + times - e, times)
        return out_ref.at[z, t, here["spin"]]

    def send(axis, distance, d, e, send_sem, recv_sem):
        size = sizes[axis]
        copy = pltpu.make_async_remote_copy(
            src_ref=in_ref if d == 0 and e == 0 else slot(d, e),
            dst_ref=slot(d, e),
            send_sem=send_sem,
            recv_sem=recv_sem,
            device_id={axis: lax.rem(here[axis] + distance, size)},
            device_id_type=MESH,
        )
        copy.start()
        return copy

    z_copies = [
        send("space", d, 0, 0, z_send.at[d], z_recv.at[d]) for d in range(1, layers)
    ]
    t_copies, c_copies = {}, []

    def pass_cores(d, e):
        for f in range(1, cores):
            c_copies.append(send("spin", f, d, e, c_send.at[d, e, f], c_recv.at[d, e, f]))

    def pass_times(d):
        for e in range(1, times):
            t_copies[d, e] = send("tm", e, d, 0, t_send.at[d, e], t_recv.at[d, e])
        pass_cores(d, 0)

    pass_times(0)
    out_ref[here["space"], here["tm"], here["spin"]] = in_ref[...]
    for d in range(1, layers):
        z_copies[d - 1].wait_recv()
        pass_times(d)
    for (d, e), copy in t_copies.items():
        copy.wait_recv()
        pass_cores(d, e)
    for copy in c_copies:
        copy.wait()
    for copy in z_copies + list(t_copies.values()):
        copy.wait_send()


def gather_all(block, layers, times, cores):
    dma = pltpu.SemaphoreType.DMA
    return pl.pallas_call(
        functools.partial(gather_kernel, layers, times, cores),
        out_shape=jax.ShapeDtypeStruct((layers, times, cores) + block.shape, BF),
        in_specs=[pl.BlockSpec(memory_space=pltpu.VMEM)],
        out_specs=pl.BlockSpec(memory_space=pltpu.VMEM),
        scratch_shapes=[
            dma((layers,)),
            dma((layers,)),
            dma((layers, times)),
            dma((layers, times)),
            dma((layers, times, cores)),
            dma((layers, times, cores)),
        ],
        compiler_params=pltpu.CompilerParams(collective_id=1, has_side_effects=True),
        name="gather_all",
    )(block)


def shift_over(array, axis, by):
    count = lax.axis_size(axis)
    return lax.ppermute(array, axis, [(i, (i + by) % count) for i in range(count)])


def halo(eigvecs):
    plane = eigvecs[:, :, :, :PLANE]
    return shift_over(plane, "space", -1)


def shards(eigvecs, links, directions, pair_list, pair_operators, perambulators):
    slices, _, _, local_sites, columns = eigvecs.shape
    plane_count = local_sites // PLANE
    layers = lax.axis_size("space")
    tm_size = lax.axis_size("tm")
    spin_size = lax.axis_size("spin")
    z_total = plane_count * layers
    scaling = 1.0 / math.sqrt(6.0 * PLANE * z_total)
    op_slots = directions.shape[0]
    z_coord = (lax.axis_index("space") * plane_count + jnp.arange(plane_count)).astype(F32)
    angles = 2.0 * math.pi / z_total * z_coord
    phases = jnp.stack([jnp.cos(angles), jnp.sin(angles)])
    above = halo(eigvecs)

    flat = links.astype(F32).reshape(slices, 3, 18, local_sites)

    partial = pl.pallas_call(
        functools.partial(local_kernel, plane_count, columns, scaling),
        out_shape=jax.ShapeDtypeStruct((slices, op_slots, columns, 2 * columns), F32),
        grid_spec=pltpu.PrefetchScalarGridSpec(
            num_scalar_prefetch=2,
            grid=(slices, op_slots),
            in_specs=[
                pl.BlockSpec((1, 2, 3, local_sites, columns), lambda t, o, d, f: (t, 0, 0, 0, 0)),
                pl.BlockSpec(
                    (1, 1, 18, local_sites),
                    lambda t, o, d, f: (t, jnp.minimum(d[o], 2), 0, 0),
                ),
            ],
            out_specs=pl.BlockSpec((1, 1, columns, 2 * columns), lambda t, o, d, f: (t, o, 0, 0)),
            scratch_shapes=[
                pltpu.VMEM((2 * columns, 3 * local_sites), BF),
                pltpu.VMEM((3, local_sites, 2 * columns), BF),
            ],
        ),
        compiler_params=pltpu.CompilerParams(vmem_limit_bytes=48 << 20),
        cost_estimate=pl.CostEstimate(
            flops=13_000_000_000, bytes_accessed=eigvecs.size * 2, transcendentals=0
        ),
        name="local_gram",
    )(directions, phases, eigvecs, flat)

    last = plane_count - 1
    rows = columns // layers
    summed = pl.pallas_call(
        functools.partial(boundary_kernel, columns, scaling),
        out_shape=jax.ShapeDtypeStruct((layers, slices, op_slots, rows, 2 * columns), F32),
        grid_spec=pltpu.PrefetchScalarGridSpec(
            num_scalar_prefetch=1,
            grid=(slices,),
            in_specs=[
                pl.BlockSpec((1, 2, 3, PLANE, columns), lambda t, d: (t, 0, 0, last, 0)),
                pl.BlockSpec((1, 1, 2, 3, 3, PLANE), lambda t, d: (t, 2, 0, 0, 0, last)),
                pl.BlockSpec((1, 2, 3, PLANE, columns), lambda t, d: (t, 0, 0, 0, 0)),
                pl.BlockSpec((1, op_slots, columns, 2 * columns), lambda t, d: (t, 0, 0, 0)),
            ],
            out_specs=pl.BlockSpec(
                (layers, 1, op_slots, rows, 2 * columns), lambda t, d: (0, t, 0, 0, 0)
            ),
        ),
        name="boundary",
    )(directions, eigvecs, links, above, partial)

    elementals, halves = reduce_rows(summed, layers)
    elementals = elementals.reshape(slices, op_slots, rows, 2, columns)
    table = gather_all(halves, layers, tm_size, spin_size)
    table = table.reshape(layers, tm_size * spin_size * slices * op_slots, rows, 2 * columns)

    position = (
        (pair_list // slices * spin_size + pair_operators // op_slots) * slices + pair_list % slices
    ) * op_slots + pair_operators % op_slots
    pair_count, count = perambulators.shape[0], perambulators.shape[1]
    spin_pair = lax.axis_index("spin") * count + jnp.arange(count)
    signs = jnp.where((spin_pair // 4 < 2) == (spin_pair % 4 < 2), 1.0, -1.0).astype(F32)
    block = (layers, 1, rows, 2 * columns)
    traces = pl.pallas_call(
        functools.partial(contract_kernel, columns, 4),
        out_shape=jax.ShapeDtypeStruct((pair_count, 2, 8, columns), F32),
        grid_spec=pltpu.PrefetchScalarGridSpec(
            num_scalar_prefetch=2,
            grid=(pair_count,),
            in_specs=[
                pl.BlockSpec(block, lambda p, pos, s: (0, pos[p, 0], 0, 0)),
                pl.BlockSpec(block, lambda p, pos, s: (0, pos[p, 1], 0, 0)),
                pl.BlockSpec((1, count, 2, columns, columns), lambda p, pos, s: (p, 0, 0, 0, 0)),
            ],
            out_specs=pl.BlockSpec((1, 2, 8, columns), lambda p, pos, s: (p, 0, 0, 0)),
        ),
        name="contract",
    )(position, signs, table, table, perambulators)
    part = jnp.sum(traces, axis=(2, 3)) / (4.0 * columns)
    if spin_size == 2:
        correlators = part + shift_over(part, "spin", 1)
    else:
        correlators = lax.psum(part, "spin")
    return (elementals, correlators)


def solution(mesh):
    return jax.shard_map(
        shards,
        mesh=mesh,
        in_specs=(
            P("tm", None, None, "space", None),
            P("tm", None, None, None, None, "space"),
            P("spin"),
            P(("space", "tm"), None),
            P(("space", "tm"), None),
            P(("space", "tm"), "spin", None, None, None),
        ),
        out_specs=(P(("ens", "tm"), "spin", "space", None, None), P(("ens", "space", "tm"), None)),
        check_vma=False,
    )
```

```python
import functools
import math

import jax
import jax.numpy as jnp
from jax import lax
from jax.experimental import pallas as pl
from jax.experimental.pallas import tpu as pltpu
from jax.sharding import PartitionSpec as P

PX = 16
PY = 16
PLANE = PX * PY
BF = jnp.bfloat16
F32 = jnp.float32
MESH = pl.DeviceIdType.MESH


def neighbour_mask(group, shift_x):
    row = lax.broadcasted_iota(jnp.int32, (group, group), 0)
    col = lax.broadcasted_iota(jnp.int32, (group, group), 1)
    if shift_x:
        col = (col // PX) * PX + lax.rem(col + 1, PX)
    return jnp.where(row == col, 1.0, 0.0).astype(BF)


def carried(links_ref, lead, offset, group, mask, real, imag):
    columns = real[0].shape[-1]
    rows = []
    for b in range(3):
        parts = []
        for part in range(2):
            for a in range(3):
                row = links_ref[lead + (part, a, pl.ds(b, 1), pl.ds(offset, group))]
                parts.append(jnp.broadcast_to(row, (group, group)) * mask)
        rows.append(jnp.concatenate(parts, axis=1))
    matrix = jnp.concatenate(rows, axis=0)
    weights = jnp.concatenate(
        [jnp.concatenate([real[a], -imag[a]], axis=1) for a in range(3)]
        + [jnp.concatenate([imag[a], real[a]], axis=1) for a in range(3)],
        axis=0,
    )
    return jnp.dot(matrix, weights, preferred_element_type=F32).astype(BF)


def gram(left, right):
    return lax.dot_general(left, right, (((0,), (0,)), ((), ())), preferred_element_type=F32)


def antihermitian(product, columns, scaling):
    real = product[:columns, :columns] - product[columns:, columns:]
    imag = product[:columns, columns:] + product[columns:, :columns]
    return jnp.concatenate(
        [(0.5 * scaling) * (real - real.T), (0.5 * scaling) * (imag + imag.T)], axis=1
    )


def ones_where(condition):
    return jnp.where(condition, 1.0, 0.0).astype(BF)


def spread(row, mask):
    return jnp.broadcast_to(row, mask.shape) * mask


def stencil(forward, backward, mask_up, mask_down):
    def block(part, a, b):
        up = forward[part * 9 + a * 3 + b : part * 9 + a * 3 + b + 1]
        down = backward[part * 9 + b * 3 + a : part * 9 + b * 3 + a + 1]
        ahead = spread(up, mask_up) if mask_up is not None else None
        behind = spread(down if part else -down, mask_down) if mask_down is not None else None
        if ahead is None:
            return behind
        return ahead if behind is None else ahead + behind

    return jnp.concatenate(
        [
            jnp.concatenate([block(part, a, b) for part in range(2) for b in range(3)], axis=1)
            for a in range(3)
        ],
        axis=0,
    )


def local_kernel(
    plane_count, columns, scaling, dirs, phases, v_ref, links_ref, out_ref, flipped, moved
):
    code = dirs[pl.program_id(1)]
    group = PLANE // 2
    groups = plane_count * 2
    sites = plane_count * PLANE
    strip = group // plane_count

    @pl.when(pl.program_id(1) == 0)
    def _():
        def step(n, carry):
            start = pl.multiple_of(n * group, group)
            for part in range(2):
                for a in range(3):
                    flipped[
                        pl.ds(part * columns, columns),
                        pl.ds(pl.multiple_of(a * sites + start, group), group),
                    ] = v_ref[0, part, a, pl.ds(start, group), :].T
            return carry

        lax.fori_loop(0, groups, step, 0)

    def weights(rows):
        real = [rows(0, a) for a in range(3)]
        imag = [rows(1, a) for a in range(3)]
        return jnp.concatenate(
            [jnp.concatenate([real[a], imag[a]], axis=1) for a in range(3)]
            + [jnp.concatenate([-imag[a], real[a]], axis=1) for a in range(3)],
            axis=0,
        )

    row = lax.broadcasted_iota(jnp.int32, (group, group), 0)
    col = lax.broadcasted_iota(jnp.int32, (group, group), 1)

    def natural(start):
        return lambda part, a: v_ref[0, part, a, pl.ds(start, group), :]

    def keep(start, value):
        value = value.astype(BF)
        for a in range(3):
            moved[a, pl.ds(start, group), :] = value[a * group : (a + 1) * group]

    @pl.when(code == 0)
    def _():
        base = (col // PX) * PX
        within = col - base
        mask_up = ones_where(row == base + lax.rem(within + PX - 1, PX))
        mask_down = ones_where(row == base + lax.rem(within + 1, PX))
        lane = lax.broadcasted_iota(jnp.int32, (18, group), 1)

        def step(n, carry):
            start = pl.multiple_of(n * group, group)
            field = links_ref[0, 0, :, pl.ds(start, group)]
            ahead = jnp.where(
                lax.rem(lane, PX) == 0,
                pltpu.roll(field, group - PX + 1, 1),
                pltpu.roll(field, 1, 1),
            )
            matrix = stencil(ahead.astype(BF), field.astype(BF), mask_up, mask_down)
            keep(start, jnp.dot(matrix, weights(natural(start)), preferred_element_type=F32))
            return carry

        lax.fori_loop(0, groups, step, 0)

    @pl.when(code == 1)
    def _():
        mask_up = ones_where(row == col - PX)
        mask_down = ones_where(row == col + PX)
        edge_row = lax.broadcasted_iota(jnp.int32, (PX, group), 0)
        edge_col = lax.broadcasted_iota(jnp.int32, (PX, group), 1)
        edge_up = ones_where(edge_row == edge_col)
        edge_down = ones_where(edge_row == edge_col - (group - PX))

        def step(plane, carry):
            base = pl.multiple_of(plane * PLANE, PLANE)
            starts = [pl.multiple_of(base + half * group, group) for half in range(2)]
            fields = [links_ref[0, 0, :, pl.ds(start, group)] for start in starts]
            turned = [pltpu.roll(field, PX, 1).astype(BF) for field in fields]
            fields = [field.astype(BF) for field in fields]
            loaded = [weights(natural(start)) for start in starts]
            for half in range(2):
                far = 1 - half
                matrix = stencil(turned[half], fields[half], mask_up, mask_down)
                edge = jnp.concatenate(
                    [
                        stencil(turned[half], fields[far], None, edge_down),
                        stencil(turned[half], fields[far], edge_up, None),
                    ],
                    axis=0,
                )
                value = jnp.dot(matrix, loaded[half], preferred_element_type=F32)
                rim = jnp.dot(edge, loaded[far], preferred_element_type=F32)
                pieces = []
                for a in range(3):
                    low, high = a * group, (a + 1) * group
                    pieces += [
                        value[low : low + PX] + rim[a * PX : (a + 1) * PX],
                        value[low + PX : high - PX],
                        value[high - PX : high] + rim[(3 + a) * PX : (4 + a) * PX],
                    ]
                keep(starts[half], jnp.concatenate(pieces, axis=0))
            return carry

        lax.fori_loop(0, plane_count, step, 0)

    @pl.when(code == 2)
    def _():
        lane = lax.broadcasted_iota(jnp.int32, (18, group), 1)
        mask_up = ones_where(row == col - strip)
        mask_down = ones_where(row == col + strip)

        per_chunk = group // strip

        def step(n, lines):
            turn = lax.rem(n, per_chunk)
            place_of = lax.rem(lane // strip + per_chunk - turn, per_chunk)
            field = lines[0]
            for z in range(1, plane_count):
                field = jnp.where(place_of == z, lines[z], field)
            field = pltpu.roll(field, lax.rem(per_chunk - turn, per_chunk) * strip, 1)
            ahead = pltpu.roll(field, strip, 1)
            matrix = stencil(ahead.astype(BF), field.astype(BF), mask_up, mask_down)
            places = [
                pl.multiple_of(z * PLANE + n * strip, strip) for z in range(plane_count)
            ]
            loaded = weights(
                lambda part, a: jnp.concatenate(
                    [v_ref[0, part, a, pl.ds(place, strip), :] for place in places], axis=0
                )
            )
            value = jnp.dot(matrix, loaded, preferred_element_type=F32).astype(BF)
            for a in range(3):
                for z, place in enumerate(places):
                    low = a * group + z * strip
                    moved[a, pl.ds(place, strip), :] = value[low : low + strip]
            return lines

        for chunk in range(groups // per_chunk):
            lines = tuple(
                pltpu.roll(
                    links_ref[0, 0, :, pl.ds(z * PLANE + chunk * group, group)],
                    z * strip % group,
                    1,
                )
                for z in range(plane_count)
            )
            lax.fori_loop(chunk * per_chunk, (chunk + 1) * per_chunk, step, lines)

    @pl.when(code == 3)
    def _():
        def step(plane, carry):
            base = pl.multiple_of(plane * PLANE, PLANE)
            cosine, sine = phases[0, plane], phases[1, plane]
            for a in range(3):
                real = v_ref[0, 0, a, pl.ds(base, PLANE), :].astype(F32)
                imag = v_ref[0, 1, a, pl.ds(base, PLANE), :].astype(F32)
                moved[a, pl.ds(base, PLANE), :] = jnp.concatenate(
                    [cosine * real + sine * imag, cosine * imag - sine * real], axis=1
                ).astype(BF)
            return carry

        lax.fori_loop(0, plane_count, step, 0)

    product = jnp.zeros((2 * columns, 2 * columns), F32)
    for a in range(3):
        product += jnp.dot(
            flipped[:, a * sites : (a + 1) * sites], moved[a], preferred_element_type=F32
        )
    scale = jnp.where(code == 3, scaling, 0.5 * scaling)
    out_ref[0, 0] = scale * jnp.concatenate(
        [
            product[:columns, :columns] + product[columns:, columns:],
            product[:columns, columns:] - product[columns:, :columns],
        ],
        axis=1,
    )


def boundary_kernel(columns, scaling, dirs, v_ref, links_ref, above_ref, part_ref, out_ref):
    op_slots = part_ref.shape[1]
    group = PLANE // 2
    split = (out_ref.shape[0],) + out_ref.shape[3:]
    for slot in range(op_slots):
        @pl.when(dirs[slot] != 2)
        def _(slot=slot):
            out_ref[:, 0, slot] = part_ref[0, slot].reshape(split).astype(out_ref.dtype)

        @pl.when(dirs[slot] == 2)
        def _(slot=slot):
            mask = neighbour_mask(group, False)
            total = jnp.zeros((2 * columns, 2 * columns), F32)
            for half in range(2):
                own = [
                    [v_ref[0, p, a, pl.ds(half * group, group), :] for a in range(3)]
                    for p in range(2)
                ]
                moved = carried(links_ref, (0, 0), half * group, group, mask, *own)
                other = jnp.concatenate(
                    [
                        jnp.concatenate(
                            [
                                above_ref[0, p, a, pl.ds(half * group, group), :]
                                for p in range(2)
                            ],
                            axis=1,
                        )
                        for a in range(3)
                    ],
                    axis=0,
                )
                total += gram(moved, other)
            whole = part_ref[0, slot] + antihermitian(total, columns, scaling)
            out_ref[:, 0, slot] = whole.reshape(split).astype(out_ref.dtype)


def contract_kernel(columns, quarter, positions, signs, source_ref, sink_ref, tau_ref, out_ref):
    def whole(ref):
        value = ref[...].astype(F32)
        return value.reshape(columns, 2 * columns).astype(BF)

    source, sink = whole(source_ref), whole(sink_ref)
    count = tau_ref.shape[1]
    sr, si = sink[:, :columns], sink[:, columns:]
    sink_block = jnp.concatenate(
        [jnp.concatenate([sr, -si], axis=1), jnp.concatenate([si, sr], axis=1)], axis=0
    )
    rr, ri = source[:, :columns], source[:, columns:]
    source_block = jnp.concatenate(
        [jnp.concatenate([rr, ri], axis=1), jnp.concatenate([-ri, rr], axis=1)], axis=0
    )
    total_real = jnp.zeros((8, columns), F32)
    total_imag = jnp.zeros((8, columns), F32)
    for first in range(0, count, 2):
        some = range(first, min(first + 2, count))
        stacked = jnp.concatenate(
            [
                jnp.concatenate([tau_ref[0, q, 0], tau_ref[0, q, 1]], axis=0)
                for q in some
            ],
            axis=1,
        )
        halfway = jnp.dot(sink_block, stacked, preferred_element_type=F32).astype(BF)
        lines = jnp.concatenate(
            [
                jnp.concatenate(
                    [
                        halfway[:columns, n * columns : (n + 1) * columns],
                        halfway[columns:, n * columns : (n + 1) * columns],
                    ],
                    axis=1,
                )
                for n in range(len(some))
            ],
            axis=0,
        )
        second = jnp.dot(lines, source_block, preferred_element_type=F32)
        for n, q in enumerate(some):
            out_real = second[n * columns : (n + 1) * columns, :columns]
            out_imag = second[n * columns : (n + 1) * columns, columns:]
            tau_real = tau_ref[0, q, 0].astype(F32)
            tau_imag = tau_ref[0, q, 1].astype(F32)
            real = out_real * tau_real + out_imag * tau_imag
            imag = out_imag * tau_real - out_real * tau_imag
            total_real += signs[q] * jnp.sum(real.reshape(-1, 8, columns), axis=0)
            total_imag += signs[q] * jnp.sum(imag.reshape(-1, 8, columns), axis=0)
    out_ref[0, 0] = total_real
    out_ref[0, 1] = total_imag


def reduce_kernel(layers, in_ref, sum_ref, half_ref, held, send_sem, recv_sem):
    me = lax.axis_index("space")
    barrier = pltpu.get_barrier_semaphore()
    for d in range(1, layers):
        pl.semaphore_signal(
            barrier, inc=1, device_id={"space": lax.rem(me + d, layers)}, device_id_type=MESH
        )
    pl.semaphore_wait(barrier, layers - 1)
    copies = []
    for d in range(1, layers):
        peer = lax.rem(me + d, layers)
        copy = pltpu.make_async_remote_copy(
            src_ref=in_ref.at[peer],
            dst_ref=held.at[d - 1],
            send_sem=send_sem.at[d - 1],
            recv_sem=recv_sem.at[d - 1],
            device_id={"space": peer},
            device_id_type=MESH,
        )
        copy.start()
        copies.append(copy)
    total = in_ref[me]
    for d in range(1, layers):
        copies[d - 1].wait_recv()
        total += held[d - 1]
    sum_ref[...] = total
    half_ref[...] = total.astype(BF)
    for copy in copies:
        copy.wait_send()


def reduce_rows(blocks, layers):
    shape = blocks.shape[1:]
    return pl.pallas_call(
        functools.partial(reduce_kernel, layers),
        out_shape=(jax.ShapeDtypeStruct(shape, F32), jax.ShapeDtypeStruct(shape, BF)),
        in_specs=[pl.BlockSpec(memory_space=pltpu.VMEM)],
        out_specs=(pl.BlockSpec(memory_space=pltpu.VMEM),) * 2,
        scratch_shapes=[
            pltpu.VMEM((layers - 1,) + shape, F32),
            pltpu.SemaphoreType.DMA((layers - 1,)),
            pltpu.SemaphoreType.DMA((layers - 1,)),
        ],
        compiler_params=pltpu.CompilerParams(collective_id=0, has_side_effects=True),
        name="reduce_rows",
    )(blocks)


def gather_kernel(
    layers, times, cores, in_ref, out_ref, z_send, z_recv, t_send, t_recv, c_send, c_recv
):
    sizes = {"space": layers, "tm": times, "spin": cores}
    here = {axis: lax.axis_index(axis) for axis in sizes}
    barrier = pltpu.get_barrier_semaphore()
    for axis, size in sizes.items():
        for d in range(1, size):
            pl.semaphore_signal(
                barrier,
                inc=1,
                device_id={axis: lax.rem(here[axis] + d, size)},
                device_id_type=MESH,
            )
    pl.semaphore_wait(barrier, layers + times + cores - 3)

    def slot(d, e):
        z = lax.rem(here["space"] + layers - d, layers)
        t = lax.rem(here["tm"] + times - e, times)
        return out_ref.at[z, t, here["spin"]]

    def send(axis, distance, d, e, send_sem, recv_sem):
        size = sizes[axis]
        copy = pltpu.make_async_remote_copy(
            src_ref=in_ref if d == 0 and e == 0 else slot(d, e),
            dst_ref=slot(d, e),
            send_sem=send_sem,
            recv_sem=recv_sem,
            device_id={axis: lax.rem(here[axis] + distance, size)},
            device_id_type=MESH,
        )
        copy.start()
        return copy

    z_copies = [
        send("space", d, 0, 0, z_send.at[d], z_recv.at[d]) for d in range(1, layers)
    ]
    t_copies, c_copies = {}, []

    def pass_cores(d, e):
        for f in range(1, cores):
            c_copies.append(send("spin", f, d, e, c_send.at[d, e, f], c_recv.at[d, e, f]))

    def pass_times(d):
        for e in range(1, times):
            t_copies[d, e] = send("tm", e, d, 0, t_send.at[d, e], t_recv.at[d, e])
        pass_cores(d, 0)

    pass_times(0)
    out_ref[here["space"], here["tm"], here["spin"]] = in_ref[...]
    for d in range(1, layers):
        z_copies[d - 1].wait_recv()
        pass_times(d)
    for (d, e), copy in t_copies.items():
        copy.wait_recv()
        pass_cores(d, e)
    for copy in c_copies:
        copy.wait()
    for copy in z_copies + list(t_copies.values()):
        copy.wait_send()


def gather_all(block, layers, times, cores):
    dma = pltpu.SemaphoreType.DMA
    return pl.pallas_call(
        functools.partial(gather_kernel, layers, times, cores),
        out_shape=jax.ShapeDtypeStruct((layers, times, cores) + block.shape, BF),
        in_specs=[pl.BlockSpec(memory_space=pltpu.VMEM)],
        out_specs=pl.BlockSpec(memory_space=pltpu.VMEM),
        scratch_shapes=[
            dma((layers,)),
            dma((layers,)),
            dma((layers, times)),
            dma((layers, times)),
            dma((layers, times, cores)),
            dma((layers, times, cores)),
        ],
        compiler_params=pltpu.CompilerParams(collective_id=1, has_side_effects=True),
        name="gather_all",
    )(block)


def shift_over(array, axis, by):
    count = lax.axis_size(axis)
    return lax.ppermute(array, axis, [(i, (i + by) % count) for i in range(count)])


def halo(eigvecs):
    plane = eigvecs[:, :, :, :PLANE]
    return shift_over(plane, "space", -1)


def shards(eigvecs, links, directions, pair_list, pair_operators, perambulators):
    slices, _, _, local_sites, columns = eigvecs.shape
    plane_count = local_sites // PLANE
    layers = lax.axis_size("space")
    tm_size = lax.axis_size("tm")
    spin_size = lax.axis_size("spin")
    z_total = plane_count * layers
    scaling = 1.0 / math.sqrt(6.0 * PLANE * z_total)
    op_slots = directions.shape[0]
    z_coord = (lax.axis_index("space") * plane_count + jnp.arange(plane_count)).astype(F32)
    angles = 2.0 * math.pi / z_total * z_coord
    phases = jnp.stack([jnp.cos(angles), jnp.sin(angles)])
    above = halo(eigvecs)

    flat = links.astype(F32).reshape(slices, 3, 18, local_sites)

    partial = pl.pallas_call(
        functools.partial(local_kernel, plane_count, columns, scaling),
        out_shape=jax.ShapeDtypeStruct((slices, op_slots, columns, 2 * columns), F32),
        grid_spec=pltpu.PrefetchScalarGridSpec(
            num_scalar_prefetch=2,
            grid=(slices, op_slots),
            in_specs=[
                pl.BlockSpec((1, 2, 3, local_sites, columns), lambda t, o, d, f: (t, 0, 0, 0, 0)),
                pl.BlockSpec(
                    (1, 1, 18, local_sites),
                    lambda t, o, d, f: (t, jnp.minimum(d[o], 2), 0, 0),
                ),
            ],
            out_specs=pl.BlockSpec((1, 1, columns, 2 * columns), lambda t, o, d, f: (t, o, 0, 0)),
            scratch_shapes=[
                pltpu.VMEM((2 * columns, 3 * local_sites), BF),
                pltpu.VMEM((3, local_sites, 2 * columns), BF),
            ],
        ),
        compiler_params=pltpu.CompilerParams(vmem_limit_bytes=48 << 20),
        cost_estimate=pl.CostEstimate(
            flops=13_000_000_000, bytes_accessed=eigvecs.size * 2, transcendentals=0
        ),
        name="local_gram",
    )(directions, phases, eigvecs, flat)

    last = plane_count - 1
    rows = columns // layers
    summed = pl.pallas_call(
        functools.partial(boundary_kernel, columns, scaling),
        out_shape=jax.ShapeDtypeStruct((layers, slices, op_slots, rows, 2 * columns), F32),
        grid_spec=pltpu.PrefetchScalarGridSpec(
            num_scalar_prefetch=1,
            grid=(slices,),
            in_specs=[
                pl.BlockSpec((1, 2, 3, PLANE, columns), lambda t, d: (t, 0, 0, last, 0)),
                pl.BlockSpec((1, 1, 2, 3, 3, PLANE), lambda t, d: (t, 2, 0, 0, 0, last)),
                pl.BlockSpec((1, 2, 3, PLANE, columns), lambda t, d: (t, 0, 0, 0, 0)),
                pl.BlockSpec((1, op_slots, columns, 2 * columns), lambda t, d: (t, 0, 0, 0)),
            ],
            out_specs=pl.BlockSpec(
                (layers, 1, op_slots, rows, 2 * columns), lambda t, d: (0, t, 0, 0, 0)
            ),
        ),
        name="boundary",
    )(directions, eigvecs, links, above, partial)

    elementals, halves = reduce_rows(summed, layers)
    elementals = elementals.reshape(slices, op_slots, rows, 2, columns)
    table = gather_all(halves, layers, tm_size, spin_size)
    table = table.reshape(layers, tm_size * spin_size * slices * op_slots, rows, 2 * columns)

    position = (
        (pair_list // slices * spin_size + pair_operators // op_slots) * slices + pair_list % slices
    ) * op_slots + pair_operators % op_slots
    pair_count, count = perambulators.shape[0], perambulators.shape[1]
    spin_pair = lax.axis_index("spin") * count + jnp.arange(count)
    signs = jnp.where((spin_pair // 4 < 2) == (spin_pair % 4 < 2), 1.0, -1.0).astype(F32)
    block = (layers, 1, rows, 2 * columns)
    traces = pl.pallas_call(
        functools.partial(contract_kernel, columns, 4),
        out_shape=jax.ShapeDtypeStruct((pair_count, 2, 8, columns), F32),
        grid_spec=pltpu.PrefetchScalarGridSpec(
            num_scalar_prefetch=2,
            grid=(pair_count,),
            in_specs=[
                pl.BlockSpec(block, lambda p, pos, s: (0, pos[p, 0], 0, 0)),
                pl.BlockSpec(block, lambda p, pos, s: (0, pos[p, 1], 0, 0)),
                pl.BlockSpec((1, count, 2, columns, columns), lambda p, pos, s: (p, 0, 0, 0, 0)),
            ],
            out_specs=pl.BlockSpec((1, 2, 8, columns), lambda p, pos, s: (p, 0, 0, 0)),
        ),
        name="contract",
    )(position, signs, table, table, perambulators)
    part = jnp.sum(traces, axis=(2, 3)) / (4.0 * columns)
    if spin_size == 2:
        correlators = part + shift_over(part, "spin", 1)
    else:
        correlators = lax.psum(part, "spin")
    return (elementals, correlators)


def solution(mesh):
    return jax.shard_map(
        shards,
        mesh=mesh,
        in_specs=(
            P("tm", None, None, "space", None),
            P("tm", None, None, None, None, "space"),
            P("spin"),
            P(("space", "tm"), None),
            P(("space", "tm"), None),
            P(("space", "tm"), "spin", None, None, None),
        ),
        out_specs=(P(("ens", "tm"), "spin", "space", None, None), P(("ens", "space", "tm"), None)),
        check_vma=False,
    )
```

```python
import functools
import math

import jax
import jax.numpy as jnp
from jax import lax
from jax.experimental import pallas as pl
from jax.experimental.pallas import tpu as pltpu
from jax.sharding import PartitionSpec as P

PX = 16
PY = 16
PLANE = PX * PY
BF = jnp.bfloat16
F32 = jnp.float32
MESH = pl.DeviceIdType.MESH


def neighbour_mask(group, shift_x):
    row = lax.broadcasted_iota(jnp.int32, (group, group), 0)
    col = lax.broadcasted_iota(jnp.int32, (group, group), 1)
    if shift_x:
        col = (col // PX) * PX + lax.rem(col + 1, PX)
    return jnp.where(row == col, 1.0, 0.0).astype(BF)


def carried(links_ref, lead, offset, group, mask, real, imag):
    columns = real[0].shape[-1]
    rows = []
    for b in range(3):
        parts = []
        for part in range(2):
            for a in range(3):
                row = links_ref[lead + (pl.ds(part * 9 + a * 3 + b, 1), pl.ds(offset, group))].astype(BF)
                parts.append(jnp.broadcast_to(row, (group, group)) * mask)
        rows.append(jnp.concatenate(parts, axis=1))
    matrix = jnp.concatenate(rows, axis=0)
    weights = jnp.concatenate(
        [jnp.concatenate([real[a], -imag[a]], axis=1) for a in range(3)]
        + [jnp.concatenate([imag[a], real[a]], axis=1) for a in range(3)],
        axis=0,
    )
    return jnp.dot(matrix, weights, preferred_element_type=F32).astype(BF)


def gram(left, right):
    return lax.dot_general(left, right, (((0,), (0,)), ((), ())), preferred_element_type=F32)


def antihermitian(product, columns, scaling):
    real = product[:columns, :columns] - product[columns:, columns:]
    imag = product[:columns, columns:] + product[columns:, :columns]
    return jnp.concatenate(
        [(0.5 * scaling) * (real - real.T), (0.5 * scaling) * (imag + imag.T)], axis=1
    )


def ones_where(condition):
    return jnp.where(condition, 1.0, 0.0).astype(BF)


def spread(row, mask):
    return jnp.broadcast_to(row, mask.shape) * mask


def stencil(forward, backward, mask_up, mask_down):
    def block(part, a, b):
        up = forward[part * 9 + a * 3 + b : part * 9 + a * 3 + b + 1]
        down = backward[part * 9 + b * 3 + a : part * 9 + b * 3 + a + 1]
        ahead = spread(up, mask_up) if mask_up is not None else None
        behind = spread(down if part else -down, mask_down) if mask_down is not None else None
        if ahead is None:
            return behind
        return ahead if behind is None else ahead + behind

    return jnp.concatenate(
        [
            jnp.concatenate([block(part, a, b) for part in range(2) for b in range(3)], axis=1)
            for a in range(3)
        ],
        axis=0,
    )


def local_kernel(
    plane_count, columns, scaling, dirs, phases, v_ref, links_ref, out_ref, flipped, moved
):
    code = dirs[pl.program_id(1)]
    group = PLANE // 2
    groups = plane_count * 2
    sites = plane_count * PLANE
    strip = group // plane_count

    @pl.when(pl.program_id(1) == 0)
    def _():
        def step(n, carry):
            start = pl.multiple_of(n * group, group)
            for part in range(2):
                for a in range(3):
                    flipped[
                        pl.ds(part * columns, columns),
                        pl.ds(pl.multiple_of(a * sites + start, group), group),
                    ] = v_ref[0, part, a, pl.ds(start, group), :].T
            return carry

        lax.fori_loop(0, groups, step, 0)

    def weights(rows):
        real = [rows(0, a) for a in range(3)]
        imag = [rows(1, a) for a in range(3)]
        return jnp.concatenate(
            [jnp.concatenate([real[a], imag[a]], axis=1) for a in range(3)]
            + [jnp.concatenate([-imag[a], real[a]], axis=1) for a in range(3)],
            axis=0,
        )

    row = lax.broadcasted_iota(jnp.int32, (group, group), 0)
    col = lax.broadcasted_iota(jnp.int32, (group, group), 1)

    def natural(start):
        return lambda part, a: v_ref[0, part, a, pl.ds(start, group), :]

    def keep(start, value):
        value = value.astype(BF)
        for a in range(3):
            moved[a, pl.ds(start, group), :] = value[a * group : (a + 1) * group]

    @pl.when(code == 0)
    def _():
        base = (col // PX) * PX
        within = col - base
        mask_up = ones_where(row == base + lax.rem(within + PX - 1, PX))
        mask_down = ones_where(row == base + lax.rem(within + 1, PX))
        lane = lax.broadcasted_iota(jnp.int32, (18, group), 1)

        def step(n, carry):
            start = pl.multiple_of(n * group, group)
            field = links_ref[0, 0, :, pl.ds(start, group)]
            ahead = jnp.where(
                lax.rem(lane, PX) == 0,
                pltpu.roll(field, group - PX + 1, 1),
                pltpu.roll(field, 1, 1),
            )
            matrix = stencil(ahead.astype(BF), field.astype(BF), mask_up, mask_down)
            keep(start, jnp.dot(matrix, weights(natural(start)), preferred_element_type=F32))
            return carry

        lax.fori_loop(0, groups, step, 0)

    @pl.when(code == 1)
    def _():
        mask_up = ones_where(row == col - PX)
        mask_down = ones_where(row == col + PX)
        edge_row = lax.broadcasted_iota(jnp.int32, (PX, group), 0)
        edge_col = lax.broadcasted_iota(jnp.int32, (PX, group), 1)
        edge_up = ones_where(edge_row == edge_col)
        edge_down = ones_where(edge_row == edge_col - (group - PX))

        def step(plane, carry):
            base = pl.multiple_of(plane * PLANE, PLANE)
            starts = [pl.multiple_of(base + half * group, group) for half in range(2)]
            fields = [links_ref[0, 0, :, pl.ds(start, group)] for start in starts]
            turned = [pltpu.roll(field, PX, 1).astype(BF) for field in fields]
            fields = [field.astype(BF) for field in fields]
            loaded = [weights(natural(start)) for start in starts]
            for half in range(2):
                far = 1 - half
                matrix = stencil(turned[half], fields[half], mask_up, mask_down)
                edge = jnp.concatenate(
                    [
                        stencil(turned[half], fields[far], None, edge_down),
                        stencil(turned[half], fields[far], edge_up, None),
                    ],
                    axis=0,
                )
                value = jnp.dot(matrix, loaded[half], preferred_element_type=F32)
                rim = jnp.dot(edge, loaded[far], preferred_element_type=F32)
                pieces = []
                for a in range(3):
                    low, high = a * group, (a + 1) * group
                    pieces += [
                        value[low : low + PX] + rim[a * PX : (a + 1) * PX],
                        value[low + PX : high - PX],
                        value[high - PX : high] + rim[(3 + a) * PX : (4 + a) * PX],
                    ]
                keep(starts[half], jnp.concatenate(pieces, axis=0))
            return carry

        lax.fori_loop(0, plane_count, step, 0)

    @pl.when(code == 2)
    def _():
        lane = lax.broadcasted_iota(jnp.int32, (18, group), 1)
        mask_up = ones_where(row == col - strip)
        mask_down = ones_where(row == col + strip)

        per_chunk = group // strip

        def step(n, lines):
            turn = lax.rem(n, per_chunk)
            place_of = lax.rem(lane // strip + per_chunk - turn, per_chunk)
            field = lines[0]
            for z in range(1, plane_count):
                field = jnp.where(place_of == z, lines[z], field)
            field = pltpu.roll(field, lax.rem(per_chunk - turn, per_chunk) * strip, 1)
            ahead = pltpu.roll(field, strip, 1)
            matrix = stencil(ahead.astype(BF), field.astype(BF), mask_up, mask_down)
            places = [
                pl.multiple_of(z * PLANE + n * strip, strip) for z in range(plane_count)
            ]
            loaded = weights(
                lambda part, a: jnp.concatenate(
                    [v_ref[0, part, a, pl.ds(place, strip), :] for place in places], axis=0
                )
            )
            value = jnp.dot(matrix, loaded, preferred_element_type=F32).astype(BF)
            for a in range(3):
                for z, place in enumerate(places):
                    low = a * group + z * strip
                    moved[a, pl.ds(place, strip), :] = value[low : low + strip]
            return lines

        for chunk in range(groups // per_chunk):
            lines = tuple(
                pltpu.roll(
                    links_ref[0, 0, :, pl.ds(z * PLANE + chunk * group, group)],
                    z * strip % group,
                    1,
                )
                for z in range(plane_count)
            )
            lax.fori_loop(chunk * per_chunk, (chunk + 1) * per_chunk, step, lines)

    @pl.when(code == 3)
    def _():
        def step(plane, carry):
            base = pl.multiple_of(plane * PLANE, PLANE)
            cosine, sine = phases[0, plane], phases[1, plane]
            for a in range(3):
                real = v_ref[0, 0, a, pl.ds(base, PLANE), :].astype(F32)
                imag = v_ref[0, 1, a, pl.ds(base, PLANE), :].astype(F32)
                moved[a, pl.ds(base, PLANE), :] = jnp.concatenate(
                    [cosine * real + sine * imag, cosine * imag - sine * real], axis=1
                ).astype(BF)
            return carry

        lax.fori_loop(0, plane_count, step, 0)

    product = jnp.zeros((2 * columns, 2 * columns), F32)
    for a in range(3):
        product += jnp.dot(
            flipped[:, a * sites : (a + 1) * sites], moved[a], preferred_element_type=F32
        )
    scale = jnp.where(code == 3, scaling, 0.5 * scaling)
    out_ref[0, 0] = scale * jnp.concatenate(
        [
            product[:columns, :columns] + product[columns:, columns:],
            product[:columns, columns:] - product[columns:, :columns],
        ],
        axis=1,
    )


def boundary_kernel(columns, scaling, dirs, v_ref, links_ref, above_ref, part_ref, out_ref):
    op_slots = part_ref.shape[1]
    group = PLANE // 2
    split = (out_ref.shape[0],) + out_ref.shape[3:]
    for slot in range(op_slots):
        @pl.when(dirs[slot] != 2)
        def _(slot=slot):
            out_ref[:, 0, slot] = part_ref[0, slot].reshape(split).astype(out_ref.dtype)

        @pl.when(dirs[slot] == 2)
        def _(slot=slot):
            mask = neighbour_mask(group, False)
            total = jnp.zeros((2 * columns, 2 * columns), F32)
            for half in range(2):
                own = [
                    [v_ref[0, p, a, pl.ds(half * group, group), :] for a in range(3)]
                    for p in range(2)
                ]
                moved = carried(links_ref, (0, 0), half * group, group, mask, *own)
                other = jnp.concatenate(
                    [
                        jnp.concatenate(
                            [
                                above_ref[0, p, a, pl.ds(half * group, group), :]
                                for p in range(2)
                            ],
                            axis=1,
                        )
                        for a in range(3)
                    ],
                    axis=0,
                )
                total += gram(moved, other)
            whole = part_ref[0, slot] + antihermitian(total, columns, scaling)
            out_ref[:, 0, slot] = whole.reshape(split).astype(out_ref.dtype)


def contract_kernel(columns, quarter, positions, signs, source_ref, sink_ref, tau_ref, out_ref):
    def whole(ref):
        value = ref[...].astype(F32)
        return value.reshape(columns, 2 * columns).astype(BF)

    source, sink = whole(source_ref), whole(sink_ref)
    count = tau_ref.shape[1]
    sr, si = sink[:, :columns], sink[:, columns:]
    sink_block = jnp.concatenate(
        [jnp.concatenate([sr, -si], axis=1), jnp.concatenate([si, sr], axis=1)], axis=0
    )
    rr, ri = source[:, :columns], source[:, columns:]
    source_block = jnp.concatenate(
        [jnp.concatenate([rr, ri], axis=1), jnp.concatenate([-ri, rr], axis=1)], axis=0
    )
    total_real = jnp.zeros((8, columns), F32)
    total_imag = jnp.zeros((8, columns), F32)
    for first in range(0, count, 2):
        some = range(first, min(first + 2, count))
        stacked = jnp.concatenate(
            [
                jnp.concatenate([tau_ref[0, q, 0], tau_ref[0, q, 1]], axis=0)
                for q in some
            ],
            axis=1,
        )
        halfway = jnp.dot(sink_block, stacked, preferred_element_type=F32).astype(BF)
        lines = jnp.concatenate(
            [
                jnp.concatenate(
                    [
                        halfway[:columns, n * columns : (n + 1) * columns],
                        halfway[columns:, n * columns : (n + 1) * columns],
                    ],
                    axis=1,
                )
                for n in range(len(some))
            ],
            axis=0,
        )
        second = jnp.dot(lines, source_block, preferred_element_type=F32)
        for n, q in enumerate(some):
            out_real = second[n * columns : (n + 1) * columns, :columns]
            out_imag = second[n * columns : (n + 1) * columns, columns:]
            tau_real = tau_ref[0, q, 0].astype(F32)
            tau_imag = tau_ref[0, q, 1].astype(F32)
            real = out_real * tau_real + out_imag * tau_imag
            imag = out_imag * tau_real - out_real * tau_imag
            total_real += signs[q] * jnp.sum(real.reshape(-1, 8, columns), axis=0)
            total_imag += signs[q] * jnp.sum(imag.reshape(-1, 8, columns), axis=0)
    out_ref[0, 0] = total_real
    out_ref[0, 1] = total_imag


def reduce_kernel(layers, in_ref, sum_ref, half_ref, held, send_sem, recv_sem):
    me = lax.axis_index("space")
    barrier = pltpu.get_barrier_semaphore()
    for d in range(1, layers):
        pl.semaphore_signal(
            barrier, inc=1, device_id={"space": lax.rem(me + d, layers)}, device_id_type=MESH
        )
    pl.semaphore_wait(barrier, layers - 1)
    copies = []
    for d in range(1, layers):
        peer = lax.rem(me + d, layers)
        copy = pltpu.make_async_remote_copy(
            src_ref=in_ref.at[peer],
            dst_ref=held.at[d - 1],
            send_sem=send_sem.at[d - 1],
            recv_sem=recv_sem.at[d - 1],
            device_id={"space": peer},
            device_id_type=MESH,
        )
        copy.start()
        copies.append(copy)
    total = in_ref[me]
    for d in range(1, layers):
        copies[d - 1].wait_recv()
        total += held[d - 1]
    sum_ref[...] = total
    half_ref[...] = total.astype(BF)
    for copy in copies:
        copy.wait_send()


def reduce_rows(blocks, layers):
    shape = blocks.shape[1:]
    return pl.pallas_call(
        functools.partial(reduce_kernel, layers),
        out_shape=(jax.ShapeDtypeStruct(shape, F32), jax.ShapeDtypeStruct(shape, BF)),
        in_specs=[pl.BlockSpec(memory_space=pltpu.VMEM)],
        out_specs=(pl.BlockSpec(memory_space=pltpu.VMEM),) * 2,
        scratch_shapes=[
            pltpu.VMEM((layers - 1,) + shape, F32),
            pltpu.SemaphoreType.DMA((layers - 1,)),
            pltpu.SemaphoreType.DMA((layers - 1,)),
        ],
        compiler_params=pltpu.CompilerParams(collective_id=0, has_side_effects=True),
        name="reduce_rows",
    )(blocks)


def gather_kernel(
    layers, times, cores, in_ref, out_ref, z_send, z_recv, t_send, t_recv, c_send, c_recv
):
    sizes = {"space": layers, "tm": times, "spin": cores}
    here = {axis: lax.axis_index(axis) for axis in sizes}
    barrier = pltpu.get_barrier_semaphore()
    for axis, size in sizes.items():
        for d in range(1, size):
            pl.semaphore_signal(
                barrier,
                inc=1,
                device_id={axis: lax.rem(here[axis] + d, size)},
                device_id_type=MESH,
            )
    pl.semaphore_wait(barrier, layers + times + cores - 3)

    def slot(d, e):
        z = lax.rem(here["space"] + layers - d, layers)
        t = lax.rem(here["tm"] + times - e, times)
        return out_ref.at[z, t, here["spin"]]

    def send(axis, distance, d, e, send_sem, recv_sem):
        size = sizes[axis]
        copy = pltpu.make_async_remote_copy(
            src_ref=in_ref if d == 0 and e == 0 else slot(d, e),
            dst_ref=slot(d, e),
            send_sem=send_sem,
            recv_sem=recv_sem,
            device_id={axis: lax.rem(here[axis] + distance, size)},
            device_id_type=MESH,
        )
        copy.start()
        return copy

    z_copies = [
        send("space", d, 0, 0, z_send.at[d], z_recv.at[d]) for d in range(1, layers)
    ]
    t_copies, c_copies = {}, []

    def pass_cores(d, e):
        for f in range(1, cores):
            c_copies.append(send("spin", f, d, e, c_send.at[d, e, f], c_recv.at[d, e, f]))

    def pass_times(d):
        for e in range(1, times):
            t_copies[d, e] = send("tm", e, d, 0, t_send.at[d, e], t_recv.at[d, e])
        pass_cores(d, 0)

    pass_times(0)
    out_ref[here["space"], here["tm"], here["spin"]] = in_ref[...]
    for d in range(1, layers):
        z_copies[d - 1].wait_recv()
        pass_times(d)
    for (d, e), copy in t_copies.items():
        copy.wait_recv()
        pass_cores(d, e)
    for copy in c_copies:
        copy.wait()
    for copy in z_copies + list(t_copies.values()):
        copy.wait_send()


def gather_all(block, layers, times, cores):
    dma = pltpu.SemaphoreType.DMA
    return pl.pallas_call(
        functools.partial(gather_kernel, layers, times, cores),
        out_shape=jax.ShapeDtypeStruct((layers, times, cores) + block.shape, BF),
        in_specs=[pl.BlockSpec(memory_space=pltpu.VMEM)],
        out_specs=pl.BlockSpec(memory_space=pltpu.VMEM),
        scratch_shapes=[
            dma((layers,)),
            dma((layers,)),
            dma((layers, times)),
            dma((layers, times)),
            dma((layers, times, cores)),
            dma((layers, times, cores)),
        ],
        compiler_params=pltpu.CompilerParams(collective_id=1, has_side_effects=True),
        name="gather_all",
    )(block)


def shift_over(array, axis, by):
    count = lax.axis_size(axis)
    return lax.ppermute(array, axis, [(i, (i + by) % count) for i in range(count)])


def halo(eigvecs):
    plane = eigvecs[:, :, :, :PLANE]
    return shift_over(plane, "space", -1)


def shards(eigvecs, links, directions, pair_list, pair_operators, perambulators):
    slices, _, _, local_sites, columns = eigvecs.shape
    plane_count = local_sites // PLANE
    layers = lax.axis_size("space")
    tm_size = lax.axis_size("tm")
    spin_size = lax.axis_size("spin")
    z_total = plane_count * layers
    scaling = 1.0 / math.sqrt(6.0 * PLANE * z_total)
    op_slots = directions.shape[0]
    z_coord = (lax.axis_index("space") * plane_count + jnp.arange(plane_count)).astype(F32)
    angles = 2.0 * math.pi / z_total * z_coord
    phases = jnp.stack([jnp.cos(angles), jnp.sin(angles)])
    above = halo(eigvecs)

    flat = links.astype(F32).reshape(slices, 3, 18, local_sites)

    partial = pl.pallas_call(
        functools.partial(local_kernel, plane_count, columns, scaling),
        out_shape=jax.ShapeDtypeStruct((slices, op_slots, columns, 2 * columns), F32),
        grid_spec=pltpu.PrefetchScalarGridSpec(
            num_scalar_prefetch=2,
            grid=(slices, op_slots),
            in_specs=[
                pl.BlockSpec((1, 2, 3, local_sites, columns), lambda t, o, d, f: (t, 0, 0, 0, 0)),
                pl.BlockSpec(
                    (1, 1, 18, local_sites),
                    lambda t, o, d, f: (t, jnp.minimum(d[o], 2), 0, 0),
                ),
            ],
            out_specs=pl.BlockSpec((1, 1, columns, 2 * columns), lambda t, o, d, f: (t, o, 0, 0)),
            scratch_shapes=[
                pltpu.VMEM((2 * columns, 3 * local_sites), BF),
                pltpu.VMEM((3, local_sites, 2 * columns), BF),
            ],
        ),
        compiler_params=pltpu.CompilerParams(vmem_limit_bytes=48 << 20),
        cost_estimate=pl.CostEstimate(
            flops=13_000_000_000, bytes_accessed=eigvecs.size * 2, transcendentals=0
        ),
        name="local_gram",
    )(directions, phases, eigvecs, flat)

    last = plane_count - 1
    rows = columns // layers
    summed = pl.pallas_call(
        functools.partial(boundary_kernel, columns, scaling),
        out_shape=jax.ShapeDtypeStruct((layers, slices, op_slots, rows, 2 * columns), F32),
        grid_spec=pltpu.PrefetchScalarGridSpec(
            num_scalar_prefetch=1,
            grid=(slices,),
            in_specs=[
                pl.BlockSpec((1, 2, 3, PLANE, columns), lambda t, d: (t, 0, 0, last, 0)),
                pl.BlockSpec((1, 1, 18, PLANE), lambda t, d: (t, 2, 0, last)),
                pl.BlockSpec((1, 2, 3, PLANE, columns), lambda t, d: (t, 0, 0, 0, 0)),
                pl.BlockSpec((1, op_slots, columns, 2 * columns), lambda t, d: (t, 0, 0, 0)),
            ],
            out_specs=pl.BlockSpec(
                (layers, 1, op_slots, rows, 2 * columns), lambda t, d: (0, t, 0, 0, 0)
            ),
        ),
        name="boundary",
    )(directions, eigvecs, flat, above, partial)

    elementals, halves = reduce_rows(summed, layers)
    elementals = elementals.reshape(slices, op_slots, rows, 2, columns)
    table = gather_all(halves, layers, tm_size, spin_size)
    table = table.reshape(layers, tm_size * spin_size * slices * op_slots, rows, 2 * columns)

    position = (
        (pair_list // slices * spin_size + pair_operators // op_slots) * slices + pair_list % slices
    ) * op_slots + pair_operators % op_slots
    pair_count, count = perambulators.shape[0], perambulators.shape[1]
    spin_pair = lax.axis_index("spin") * count + jnp.arange(count)
    signs = jnp.where((spin_pair // 4 < 2) == (spin_pair % 4 < 2), 1.0, -1.0).astype(F32)
    block = (layers, 1, rows, 2 * columns)
    traces = pl.pallas_call(
        functools.partial(contract_kernel, columns, 4),
        out_shape=jax.ShapeDtypeStruct((pair_count, 2, 8, columns), F32),
        grid_spec=pltpu.PrefetchScalarGridSpec(
            num_scalar_prefetch=2,
            grid=(pair_count,),
            in_specs=[
                pl.BlockSpec(block, lambda p, pos, s: (0, pos[p, 0], 0, 0)),
                pl.BlockSpec(block, lambda p, pos, s: (0, pos[p, 1], 0, 0)),
                pl.BlockSpec((1, count, 2, columns, columns), lambda p, pos, s: (p, 0, 0, 0, 0)),
            ],
            out_specs=pl.BlockSpec((1, 2, 8, columns), lambda p, pos, s: (p, 0, 0, 0)),
        ),
        name="contract",
    )(position, signs, table, table, perambulators)
    part = jnp.sum(traces, axis=(2, 3)) / (4.0 * columns)
    if spin_size == 2:
        correlators = part + shift_over(part, "spin", 1)
    else:
        correlators = lax.psum(part, "spin")
    return (elementals, correlators)


def solution(mesh):
    return jax.shard_map(
        shards,
        mesh=mesh,
        in_specs=(
            P("tm", None, None, "space", None),
            P("tm", None, None, None, None, "space"),
            P("spin"),
            P(("space", "tm"), None),
            P(("space", "tm"), None),
            P(("space", "tm"), "spin", None, None, None),
        ),
        out_specs=(P(("ens", "tm"), "spin", "space", None, None), P(("ens", "space", "tm"), None)),
        check_vma=False,
    )
```
